32 devices in a mesh: groups: 2 (over y), seq: 4 (over z), inner: 2 (over x), batch: 2 (over core).
Axes of the slice: x: 2, y: 2, z: 4, core: 2. Of those that a mesh axis runs over, the one named last changes fastest.
Arguments:
- queries: bfloat16 [4, 2048, 256], P(('groups', 'batch'), ('seq', 'inner')), parts along dimension 0, may hold values from -6 to 6
- keys: bfloat16 [4, 2048, 256], P(('groups', 'batch'), ('seq', 'inner')), parts along dimension 0, may hold values from -6 to 6
- values: bfloat16 [4, 2048, 256], P(('groups', 'batch'), ('seq', 'inner')), parts along dimension 0, may hold values from -6 to 6
- rates: float32 [4, 2048], P(('groups', 'batch'), ('seq', 'inner')), parts along dimension 0, may hold values from 0.05 to 1
- video_start: int32 [4], P(('groups', 'batch')), parts along dimension 0, may hold values from 0 to 511
- span_len: int32 [4, 4], P(('groups', 'batch'), 'seq'), parts along dimension 0, may hold values from 256 to 512, as said below
- init_weights: float32 [3, 256, 256], replicated, may hold values from -0.375 to 0.375
Outputs:
- outputs: bfloat16 [4, 2048, 256], P(('groups', 'batch'), ('seq', 'inner')), parts along dimension 0
- final_weights: float32 [4, 3, 256, 256], P(('groups', 'batch'), None, 'seq'), parts along dimension 0
The draws below stay inside these ranges and needn't reach their ends.
There are 2 independent parts, one for each index of `groups`. The reference program is written for one: setup_inputs(seed, part) draws one part's arguments, and reference() takes and returns one part's arrays. A program takes and returns all parts, laid end to end along the dimension named above; an argument that names none is the same for every part. Nothing has to cross between parts.
Inputs may be any that keep to these rules, and one draw needn't show every extreme that they name: Every video has at least one span with span_len equal to 512.
All inputs are finite; a program needn't handle non-finite values.
Results may differ from the reference program's by a relative error of at most 0.015.
Values may be sent and summed in bfloat16 or wider, within the bound.
A program may use at most 64 MiB of HBM per device.

```python
import math
import jax
import jax.numpy as jnp
from jax import lax

HEAD = 256
HIDDEN_SIZE = 256
TOK_DEV = 256
NS_STEPS = 5
SPAN = 512
LENGTH = 2048
VIDEOS = 2
N_SEQ = 4
N_INNER = 2


def draw_span_len(key, part):
    drawn_len = jax.random.randint(jax.random.fold_in(key, 11), (VIDEOS, N_SEQ), SPAN // 2, SPAN + 1)
    chosen = jax.random.randint(jax.random.fold_in(key, 12), (VIDEOS, 1), 0, N_SEQ)
    full_mask = jnp.arange(N_SEQ, dtype=jnp.int32)[None, :] == chosen
    return jnp.where(full_mask, SPAN, drawn_len).astype(jnp.int32)


def levels(rng, dims, cuts, low, top_value):
    level, own = 1.0, jax.random.fold_in(rng, 6)
    for dim, blocks in cuts:
        steps = jnp.exp(jax.random.uniform(jax.random.fold_in(own, dim), (blocks,), jnp.float32, low / len(cuts), top_value / len(cuts)))
        level = level * jnp.repeat(steps, dims[dim] // blocks).reshape([-1 if axis == dim else 1 for axis in range(len(dims))])
    return level


def centred(rng, extent, scale, bound, cuts=(), kind=jnp.bfloat16):
    loudness = levels(rng, extent, cuts, -0.22, 0.18) if cuts else 1.0
    values = jax.random.normal(rng, extent, jnp.float32) * scale * loudness
    return jnp.minimum(jnp.maximum(values, -bound), bound).astype(kind)


def setup_inputs(seed: int = 0, part: int = 0) -> dict:
    arg_keys = jax.random.split(jax.random.key(seed), 8)
    own_keys = jax.random.split(jax.random.fold_in(arg_keys[7], part), 8)
    return {
        "queries": centred(own_keys[0], (VIDEOS, LENGTH, HEAD), 1.0, 6.0, ((0, 2), (1, 8))),
        "keys": centred(own_keys[1], (VIDEOS, LENGTH, HEAD), 1.0, 6.0, ((0, 2), (1, 8))),
        "values": centred(own_keys[2], (VIDEOS, LENGTH, HEAD), 1.0, 6.0, ((0, 2), (1, 8))),
        "rates": jnp.clip(jnp.exp(math.log(1.0) - 2.9957323 * jax.random.uniform(own_keys[3], (VIDEOS, LENGTH), jnp.float32) ** levels(own_keys[3], (VIDEOS, LENGTH), ((0, 2), (1, 8)), -0.2, 0.2)), 0.05, 1.0),
        "video_start": jax.random.randint(own_keys[4], (VIDEOS,), 0, SPAN).astype(jnp.int32),
        "span_len": draw_span_len(jax.random.fold_in(jax.random.fold_in(arg_keys[7], part), 71), part),
        "init_weights": centred(arg_keys[6], (3, HEAD, HIDDEN_SIZE), HEAD ** -0.5, 0.375, (), jnp.float32),
    }


step_size = 0.1
norm_eps = 1e-07
column_eps = 1e-06

def swish_parts(pre_act):
    sigma = jax.nn.sigmoid(pre_act)
    return (pre_act * sigma, sigma * (1.0 + pre_act * (1.0 - sigma)))

def apply_net(rows, half_weights):
    gate_pre = jnp.dot(rows, half_weights[0], preferred_element_type=jnp.float32)
    up_pre = jnp.dot(rows, half_weights[1], preferred_element_type=jnp.float32)
    active_part, unused_slope = swish_parts(gate_pre)
    hidden = (active_part * up_pre).astype(jnp.bfloat16)
    contract = (((1,), (1,)), ((), ()))
    return lax.dot_general(hidden, half_weights[2], contract, preferred_element_type=jnp.float32).astype(jnp.bfloat16)

def key_grads(key_rows, value_rows, weight, half_weights):
    gate_pre = jnp.dot(key_rows, half_weights[0], preferred_element_type=jnp.float32)
    up_pre = jnp.dot(key_rows, half_weights[1], preferred_element_type=jnp.float32)
    active_part, slope_term = swish_parts(gate_pre)
    hidden = (active_part * up_pre).astype(jnp.bfloat16)
    neg_values = (-(weight[:, None] * value_rows.astype(jnp.float32))).astype(jnp.bfloat16)
    back_grad = jnp.dot(neg_values, half_weights[2], preferred_element_type=jnp.float32)
    d_upper = (back_grad * active_part).astype(jnp.bfloat16)
    d_gate = (back_grad * up_pre * slope_term).astype(jnp.bfloat16)
    contract = (((0,), (0,)), ((), ()))
    grad_one = lax.dot_general(key_rows, d_gate, contract, preferred_element_type=jnp.float32)
    grad_three = lax.dot_general(key_rows, d_upper, contract, preferred_element_type=jnp.float32)
    grad_two = lax.dot_general(neg_values, hidden, contract, preferred_element_type=jnp.float32)
    return jnp.stack([grad_one, grad_three, grad_two])

def newton(grad):
    scale = jnp.sqrt(jnp.sum(grad * grad))
    iterate = grad / (scale + norm_eps)
    for unused in range(NS_STEPS):
        gram = jnp.dot(iterate, iterate.T, precision=lax.Precision.HIGHEST, preferred_element_type=jnp.float32)
        iterate = 1.5 * iterate - 0.5 * jnp.dot(gram, iterate, precision=lax.Precision.HIGHEST, preferred_element_type=jnp.float32)
    return iterate.astype(jnp.bfloat16)

def renorm(before, moved):
    old_norm = jnp.sqrt(lax.optimization_barrier(jnp.sum(before * before, axis=1, keepdims=True)) + column_eps)
    new_norm = jnp.sqrt(lax.optimization_barrier(jnp.sum(moved * moved, axis=1, keepdims=True)) + column_eps)
    return moved * (old_norm / new_norm)

def reference(queries, keys, values, rates, video_start, span_len, init_weights):

    def one_video(pieces):
        query_all, key_all, value_all, rate_all, begin, lengths = pieces

        def span_step(state, span_pieces):
            query_rows, key_rows, value_rows, rate_rows, length, span_index = span_pieces
            half_weights = state.astype(jnp.bfloat16)
            out_rows = apply_net(query_rows, half_weights)
            within = jnp.arange(SPAN, dtype=jnp.int32)
            position = span_index * SPAN + within
            valid = ((position >= begin) & (within < length)).astype(jnp.float32)
            weight = rate_rows * valid
            total = jnp.zeros(state.shape, jnp.float32)
            for shard in range(N_INNER):
                lower = shard * TOK_DEV
                partial_value = key_grads(key_rows[lower:lower + TOK_DEV], value_rows[lower:lower + TOK_DEV], weight[lower:lower + TOK_DEV], half_weights)
                rounded = lax.optimization_barrier(partial_value.astype(jnp.bfloat16))
                total = total + rounded.astype(jnp.float32)
            ortho = jnp.stack([newton(total[which]) for which in range(3)])
            new_state = renorm(state, state - step_size * ortho.astype(jnp.float32))
            return (new_state, out_rows)
        final_state, outs = lax.scan(span_step, init_weights, (query_all.reshape(N_SEQ, SPAN, HEAD), key_all.reshape(N_SEQ, SPAN, HEAD), value_all.reshape(N_SEQ, SPAN, HEAD), rate_all.reshape(N_SEQ, SPAN), lengths, jnp.arange(N_SEQ, dtype=jnp.int32)))
        return (outs.reshape(LENGTH, HEAD), final_state)
    outputs, final_weights = lax.map(one_video, (queries, keys, values, rates, video_start, span_len))
    return (outputs, final_weights)
```

```python
import functools

import jax
import jax.numpy as jnp
from jax import lax
from jax.experimental import pallas as pl
from jax.experimental.pallas import tpu as pltpu
from jax.sharding import PartitionSpec as P

NS_STEPS = 5
MESH = pl.DeviceIdType.MESH
step_size = 0.1
norm_eps = 1e-07
column_eps = 1e-06
half_root = 0.5**0.5
F32, BF16 = jnp.float32, jnp.bfloat16


def dot(a, b, ca, cb):
    return lax.dot_general(a, b, (((ca,), (cb,)), ((), ())), preferred_element_type=F32)


def sigmoid(g):
    return 0.5 + 0.5 * jnp.tanh(0.5 * g)


def apply_net(rows, w1, w3, w2):
    gate = dot(rows, w1, 1, 0)
    up = dot(rows, w3, 1, 0)
    hidden = (gate * sigmoid(gate) * up).astype(BF16)
    return dot(hidden, w2, 1, 1).astype(BF16)


def span_grads(k, nv, ws, scales):
    gate = dot(k, ws[0], 1, 0) * scales[0]
    up = dot(k, ws[1], 1, 0) * scales[1]
    back = dot(nv, ws[2], 1, 0) * scales[2]
    s = sigmoid(gate)
    active = gate * s
    hidden = (active * up).astype(BF16)
    d_up = (back * active).astype(BF16)
    d_gate = (back * up * (s + active - active * s)).astype(BF16)
    return [dot(k, d_gate, 0, 0), dot(k, d_up, 0, 0), dot(nv, hidden, 0, 0)]


def newton(grads):
    size = grads[0].shape[0]
    at = [lax.broadcasted_iota(jnp.int32, (size, size), d) for d in range(2)]
    eye = jnp.where(at[0] == at[1], 1.5, 0.0).astype(F32)
    xs = [g.astype(BF16) for g in grads]
    scales = [
        half_root / (jnp.sqrt(jnp.sum(g * g, keepdims=True)) + norm_eps) for g in grads
    ]
    factors = [(dot(x, x, 1, 1) * (s * s) - eye).astype(BF16) for x, s in zip(xs, scales)]
    ys = [dot(f, x, 1, 0) * s for f, x, s in zip(factors, xs, scales)]
    for unused in range(1, NS_STEPS):
        xs = [y.astype(BF16) for y in ys]
        factors = [(dot(x, x, 1, 1) - eye).astype(BF16) for x in xs]
        ys = [dot(f, x, 1, 0) for f, x in zip(factors, xs)]
    sign = -1.0 if NS_STEPS % 2 == 0 else 1.0
    return ys if sign > 0 else [-y for y in ys]


def kernel(
    n, m, nb, start_ref, len_ref, key_ref, value_ref, rate_ref, q_ref, init_ref, out_ref, final_ref,
    kv, queue, outs, halves, state, root, grad, fin, val_v, rate_v, q_v, nv_v,
    in_sem, kv_send, kv_recv, q_send, q_recv, h_send, h_recv, o_send, o_recv, f_send, f_recv,
    go, qgo,
):
    z, x, b = lax.axis_index("seq"), lax.axis_index("inner"), lax.axis_index("batch")
    tok, head = value_ref.shape
    rows = final_ref.shape[1]

    def master_of(v):
        return lax.rem(v, m), (n // 2) * (1 - lax.rem(v, 2))

    other = lax.rem(b + 1, nb)
    served = lax.rem(b + nb - 1, nb)
    mx, mz = master_of(b)
    sx, sz = master_of(served)
    is_master = (x == mx) & (z == mz)
    is_source = jnp.logical_not(is_master)
    is_server = (x == sx) & (z == sz)
    master = {"inner": mx, "seq": mz}
    server = {"inner": mx, "seq": mz, "batch": other}

    def same_side(lower):
        return (lower >= 0) & (lower + 1 < n) & ((lower + 1 < mz) | (lower > mz))

    has_next, has_prev = same_side(z), same_side(z - 1)
    upper = z > mz

    barrier = pltpu.get_barrier_semaphore()

    def greet(where):
        pl.semaphore_signal(barrier, inc=1, device_id=where, device_id_type=MESH)

    @pl.when(is_master)
    def _():
        @pl.loop(0, n)
        def _(c):
            for r in range(m):
                pl.when((c != mz) | (r != mx))(lambda: greet({"seq": c, "inner": r}))
        greet(server)

    @pl.when(is_server)
    def _():
        @pl.loop(0, n)
        def _(c):
            for r in range(m):
                greet({"seq": c, "inner": r, "batch": served})

    pl.when(has_prev)(lambda: greet({"seq": z - 1}))

    def fetch(src, dst, i):
        return pltpu.make_async_copy(src, dst, in_sem.at[i])

    get_val = fetch(value_ref, val_v, 0)
    get_rate = fetch(rate_ref, rate_v, 1)
    get_q = fetch(q_ref, q_v, 2)
    get_init = fetch(init_ref, state, 3)
    get_key = fetch(key_ref, kv.at[mz, mx, 0], 4)
    get_val.start()
    get_rate.start()
    pl.when(is_master)(get_key.start)
    pl.when(z == 0)(get_q.start)
    pl.when((z == 0) | is_master)(get_init.start)

    within = lax.broadcasted_iota(jnp.int32, (1, tok), 1) + x * tok
    position = within + z * (tok * m)
    valid = ((position >= start_ref[0]) & (within < len_ref[0, 0])).astype(F32)
    get_rate.wait()
    weight = rate_v[...] * valid
    eye = lax.broadcasted_iota(jnp.int32, (tok, tok), 0) == lax.broadcasted_iota(
        jnp.int32, (tok, tok), 1
    )
    column = jnp.sum(jnp.where(eye, weight, 0.0), axis=1, keepdims=True)
    get_val.wait()
    neg = (-(column * val_v[...].astype(F32))).astype(BF16)
    nv_v[...] = neg

    pl.semaphore_wait(
        barrier,
        1 + is_source.astype(jnp.int32) + is_server.astype(jnp.int32) + has_next.astype(jnp.int32),
    )

    def copy(src, dst, send, recv, where):
        return pltpu.make_async_remote_copy(src, dst, send, recv, where, MESH)

    give_k = copy(key_ref, kv.at[z, x, 0], kv_send.at[0], kv_recv.at[z, x, 0], master)
    give_nv = copy(nv_v, kv.at[z, x, 1], kv_send.at[1], kv_recv.at[z, x, 1], master)
    give_q = copy(q_ref, queue.at[z, x], q_send, q_recv.at[z, x], server)

    def take(c, r, j):
        return copy(kv.at[c, r, j], kv.at[c, r, j], kv_send.at[j], kv_recv.at[c, r, j], master)

    def give_half(c):
        return copy(halves.at[c], halves.at[c], h_send.at[c], h_recv.at[c], server)

    def give_out(c, r):
        where = {"seq": c, "inner": r, "batch": served}
        return copy(outs.at[c, r], out_ref, o_send.at[c, r], o_recv, where)

    def give_final(c, r, i):
        mine = pl.ds(pl.multiple_of(c * rows, rows), rows)
        where = {"seq": c, "inner": r}
        return copy(fin.at[i, mine], final_ref.at[i], f_send.at[c, r, i], f_recv.at[i], where)

    @pl.when(is_source)
    def _():
        pl.when(has_prev)(lambda: pl.semaphore_wait(go, 1))
        give_k.start()
        give_nv.start()

        @pl.when(has_next)
        def _():
            pl.semaphore_signal(go, inc=1, device_id={"seq": z + 1}, device_id_type=MESH)
            pl.when(upper)(lambda: pl.semaphore_wait(qgo, 1))

    @pl.when(z > 0)
    def _():
        give_q.start()

        @pl.when(has_prev & upper)
        def _():
            pl.semaphore_signal(qgo, inc=1, device_id={"seq": z - 1}, device_id_type=MESH)

    pl.when((z == 0) | is_master)(get_init.wait)

    @pl.when(z == 0)
    def _():
        get_q.wait()
        out_ref[...] = apply_net(q_v[...], *[state[i].astype(BF16) for i in range(3)])

    def sums(i):
        w = state[i]
        after = jnp.sum(w * w, axis=0, keepdims=True)
        scale = root[i] * lax.rsqrt(after + column_eps)
        total = after * (scale * scale) + column_eps
        root[i] = total * lax.rsqrt(total)
        return scale

    @pl.when(is_master)
    def _():
        for i in range(3):
            w = state[i]
            root[i] = jnp.sqrt(jnp.sum(w * w, axis=0, keepdims=True) + column_eps)
        kv[mz, mx, 1] = nv_v[...]
        get_key.wait()

        @pl.loop(0, n)
        def _(c):
            for r in range(m):
                for j in range(2):
                    pl.when((c != mz) | (r != mx))(lambda: take(c, r, j).wait_recv())
            scales = [sums(i) for i in range(3)]
            ws = [state[i].astype(BF16) for i in range(3)]
            k = kv[c, :, 0].reshape(m * tok, head)
            nv = kv[c, :, 1].reshape(m * tok, head)
            for i, g in enumerate(span_grads(k, nv, ws, scales)):
                grad[i] = g
            for i in range(3):
                w = state[i] * scales[i]
                state[i] = w
                halves[c, i] = w.astype(BF16)
            ys = newton([grad[i] for i in range(3)])
            pl.when(c > 0)(lambda: give_half(c).start())
            for i in range(3):
                state[i] = state[i] + (step_size / half_root) * ys[i]

        for i in range(3):
            fin[i] = (state[i] * sums(i)).astype(BF16)

        @pl.loop(0, n)
        def _(d):
            c = n - 1 - d
            for r in range(m):
                for i in range(3):
                    pl.when((c != mz) | (r != mx))(lambda: give_final(c, r, i).start())

        mine = pl.ds(pl.multiple_of(z * rows, rows), rows)
        final_ref[...] = fin[:, mine, :]

        @pl.loop(0, n)
        def _(c):
            for r in range(m):
                for i in range(3):
                    pl.when((c != mz) | (r != mx))(lambda: give_final(c, r, i).wait_send())
            pl.when(c > 0)(lambda: give_half(c).wait_send())

    @pl.when(is_server)
    def _():
        @pl.loop(1, n)
        def _(c):
            for r in range(m):
                copy(queue.at[c, r], queue.at[c, r], q_send, q_recv.at[c, r], server).wait_recv()
            give_half(c).wait_recv()
            ws = [halves[c, i] for i in range(3)]
            for r in range(m):
                outs[c, r] = apply_net(queue[c, r], *ws)
                give_out(c, r).start()

        @pl.loop(1, n)
        def _(c):
            for r in range(m):
                give_out(c, r).wait_send()

    @pl.when(is_source)
    def _():
        give_k.wait_send()
        give_nv.wait_send()
        for i in range(3):
            give_final(0, 0, i).wait_recv()

    @pl.when(z > 0)
    def _():
        give_q.wait_send()
        give_out(0, 0).wait_recv()


def finish(out_ref, final_ref, out_hbm, final_hbm, wide, sem):
    first = pltpu.make_async_copy(out_ref, out_hbm, sem.at[0])
    first.start()
    wide[...] = final_ref[...].astype(F32)
    second = pltpu.make_async_copy(wide, final_hbm, sem.at[1])
    second.start()
    first.wait()
    second.wait()


def per_device(queries, keys, values, rates, video_start, span_len, init_weights):
    tok, head = queries.shape[1:]
    n, m, nb = lax.axis_size("seq"), lax.axis_size("inner"), lax.axis_size("batch")
    hidden = init_weights.shape[2]
    rows = init_weights.shape[1] // n
    vm = pl.BlockSpec(memory_space=pltpu.VMEM)
    sm = pl.BlockSpec(memory_space=pltpu.SMEM)
    hbm = pl.BlockSpec(memory_space=pl.ANY)
    dma = pltpu.SemaphoreType.DMA
    out, final = pl.pallas_call(
        functools.partial(kernel, n, m, nb),
        out_shape=(
            jax.ShapeDtypeStruct((tok, head), BF16),
            jax.ShapeDtypeStruct((3, rows, hidden), BF16),
        ),
        in_specs=[sm, sm, hbm, hbm, hbm, hbm, hbm],
        out_specs=(vm, vm),
        scratch_shapes=[
            pltpu.VMEM((n, m, 2, tok, head), BF16),
            pltpu.VMEM((n, m, tok, head), BF16),
            pltpu.VMEM((n, m, tok, head), BF16),
            pltpu.VMEM((n,) + init_weights.shape, BF16),
            pltpu.VMEM(init_weights.shape, F32),
            pltpu.VMEM((3, 1, hidden), F32),
            pltpu.VMEM(init_weights.shape, F32),
            pltpu.VMEM(init_weights.shape, BF16),
            pltpu.VMEM((tok, head), BF16),
            pltpu.VMEM((1, tok), F32),
            pltpu.VMEM((tok, head), BF16),
            pltpu.VMEM((tok, head), BF16),
            dma((5,)),
            dma((2,)),
            dma((n, m, 2)),
            dma(()),
            dma((n, m)),
            dma((n,)),
            dma((n,)),
            dma((n, m)),
            dma(()),
            dma((n, m, 3)),
            dma((3,)),
            pltpu.SemaphoreType.REGULAR,
            pltpu.SemaphoreType.REGULAR,
        ],
        compiler_params=pltpu.CompilerParams(collective_id=0, has_side_effects=True),
    )(video_start, span_len, keys[0], values[0], rates, queries[0], init_weights)
    out, final = pl.pallas_call(
        finish,
        out_shape=(
            jax.ShapeDtypeStruct((tok, head), BF16),
            jax.ShapeDtypeStruct((3, rows, hidden), F32),
        ),
        in_specs=[vm, vm],
        out_specs=(hbm, hbm),
        scratch_shapes=[pltpu.VMEM((3, rows, hidden), F32), dma((2,))],
    )(out, final)
    return out[None], final[None]


def solution(mesh):
    in_specs = (
        P(("groups", "batch"), ("seq", "inner"), None),
        P(("groups", "batch"), ("seq", "inner"), None),
        P(("groups", "batch"), ("seq", "inner"), None),
        P(("groups", "batch"), ("seq", "inner")),
        P(("groups", "batch")),
        P(("groups", "batch"), "seq"),
        P(),
    )
    out_specs = (
        P(("groups", "batch"), ("seq", "inner"), None),
        P(("groups", "batch"), None, "seq", None),
    )
    return jax.shard_map(
        per_device, mesh=mesh, in_specs=in_specs, out_specs=out_specs, check_vma=False
    )
```

```python
import functools

import jax
import jax.numpy as jnp
from jax import lax
from jax.experimental import pallas as pl
from jax.experimental.pallas import tpu as pltpu
from jax.sharding import PartitionSpec as P

NS_STEPS = 5
MESH = pl.DeviceIdType.MESH
step_size = 0.1
norm_eps = 1e-07
column_eps = 1e-06
half_root = 0.5**0.5
F32, BF16 = jnp.float32, jnp.bfloat16


def dot(a, b, ca, cb):
    return lax.dot_general(a, b, (((ca,), (cb,)), ((), ())), preferred_element_type=F32)


def sigmoid(g):
    return 0.5 + 0.5 * jnp.tanh(0.5 * g)


def apply_net(rows, w1, w3, w2):
    gate = dot(rows, w1, 1, 0)
    up = dot(rows, w3, 1, 0)
    hidden = (gate * sigmoid(gate) * up).astype(BF16)
    return dot(hidden, w2, 1, 1).astype(BF16)


def span_grads(k, nv, ws, scales):
    gate = dot(k, ws[0], 1, 0) * scales[0]
    up = dot(k, ws[1], 1, 0) * scales[1]
    back = dot(nv, ws[2], 1, 0) * scales[2]
    s = sigmoid(gate)
    active = gate * s
    hidden = (active * up).astype(BF16)
    d_up = (back * active).astype(BF16)
    d_gate = (back * up * (s + active - active * s)).astype(BF16)
    return [dot(k, d_gate, 0, 0), dot(k, d_up, 0, 0), dot(nv, hidden, 0, 0)]


def newton(grads):
    size = grads[0].shape[0]
    at = [lax.broadcasted_iota(jnp.int32, (size, size), d) for d in range(2)]
    eye = jnp.where(at[0] == at[1], 1.5, 0.0).astype(F32)
    xs = [g.astype(BF16) for g in grads]
    scales = [
        half_root / (jnp.sqrt(jnp.sum(g * g, keepdims=True)) + norm_eps) for g in grads
    ]
    factors = [(dot(x, x, 1, 1) * (s * s) - eye).astype(BF16) for x, s in zip(xs, scales)]
    ys = [dot(f, x, 1, 0) * s for f, x, s in zip(factors, xs, scales)]
    for unused in range(1, NS_STEPS):
        xs = [y.astype(BF16) for y in ys]
        factors = [(dot(x, x, 1, 1) - eye).astype(BF16) for x in xs]
        ys = [dot(f, x, 1, 0) for f, x in zip(factors, xs)]
    sign = -1.0 if NS_STEPS % 2 == 0 else 1.0
    return ys if sign > 0 else [-y for y in ys]


def kernel(
    n, m, nb, start_ref, len_ref, key_ref, value_ref, rate_ref, q_ref, init_ref, out_ref, final_ref,
    kv, queue, outs, halves, state, root, grad, fin, val_v, rate_v, q_v, nv_v, first_v, len_v,
    in_sem, kv_send, kv_recv, pass_send, q_send, q_recv, h_send, h_recv, o_send, o_recv, f_send, f_recv,
    go, qgo,
):
    z, x, b = lax.axis_index("seq"), lax.axis_index("inner"), lax.axis_index("batch")
    tok, head = value_ref.shape
    rows = final_ref.shape[1]

    def home(v):
        return (n // 2) * (1 - lax.rem(v, 2))

    other = lax.rem(b + 1, nb)
    served = lax.rem(b + nb - 1, nb)
    mz, sz = home(b), home(served)
    is_master, is_server = z == mz, z == sz
    is_source = jnp.logical_not(is_master)
    upper = z > mz

    def same_side(lower):
        return (lower >= 0) & (lower + 1 < n) & ((lower + 1 < mz) | (lower > mz))

    has_next, has_prev = same_side(z), same_side(z - 1)
    twins = [lax.rem(x + d, m) for d in range(1, m)]

    barrier = pltpu.get_barrier_semaphore()

    def greet(where):
        pl.semaphore_signal(barrier, inc=1, device_id=where, device_id_type=MESH)

    @pl.when(is_master)
    def _():
        for r in twins:
            greet({"inner": r})
        for r in range(m):
            greet({"inner": r, "batch": other})

    @pl.when(is_server)
    def _():
        @pl.loop(0, n)
        def _(c):
            greet({"seq": c, "batch": served})

    pl.when(has_prev)(lambda: greet({"seq": z - 1}))

    def fetch(src, dst, i):
        return pltpu.make_async_copy(src, dst, in_sem.at[i])

    get_val = fetch(value_ref, val_v, 0)
    get_rate = fetch(rate_ref, rate_v, 1)
    get_q = fetch(q_ref, q_v, 2)
    get_init = fetch(init_ref, state, 3)
    get_key = fetch(key_ref, kv.at[mz, x, 0], 4)
    get_first = fetch(start_ref, first_v, 5)
    get_len = fetch(len_ref, len_v, 6)
    get_first.start()
    get_len.start()
    get_rate.start()
    get_val.start()
    pl.when(is_master)(get_key.start)
    pl.when(z == 0)(get_q.start)
    pl.when((z == 0) | is_master)(get_init.start)

    within = lax.broadcasted_iota(jnp.int32, (1, tok), 1) + x * tok
    position = within + z * (tok * m)
    eye = lax.broadcasted_iota(jnp.int32, (tok, tok), 0) == lax.broadcasted_iota(
        jnp.int32, (tok, tok), 1
    )
    get_first.wait()
    get_len.wait()
    get_rate.wait()
    valid = ((position >= first_v[...]) & (within < len_v[...])).astype(F32)
    weight = rate_v[...] * valid
    column = jnp.sum(jnp.where(eye, weight, 0.0), axis=1, keepdims=True)
    get_val.wait()
    nv_v[...] = (-(column * val_v[...].astype(F32))).astype(BF16)

    pl.semaphore_wait(
        barrier,
        1
        + is_master.astype(jnp.int32) * (m - 1)
        + is_server.astype(jnp.int32) * m
        + has_next.astype(jnp.int32),
    )

    def copy(src, dst, send, recv, where):
        return pltpu.make_async_remote_copy(src, dst, send, recv, where, MESH)

    def give(i, where, slot):
        src = key_ref if i == 0 else nv_v
        return copy(src, kv.at[z, x, i], kv_send.at[slot, i], kv_recv.at[z, x, i], where)

    def take(c, r, i):
        block = kv.at[c, r, i]
        return copy(block, block, kv_send.at[0, i], kv_recv.at[c, r, i], {"seq": mz})

    def forward(c, i, r, slot):
        block = kv.at[c, x, i]
        where = {"inner": r, "batch": served}
        return copy(block, block, pass_send.at[c, i, slot], kv_recv.at[c, x, i], where)

    server = {"seq": mz, "batch": other}
    give_q = copy(q_ref, queue.at[z], q_send, q_recv.at[z], server)

    def give_half(c):
        return copy(halves.at[c], halves.at[c], h_send.at[c], h_recv.at[c], server)

    def give_out(c):
        where = {"seq": c, "batch": served}
        return copy(outs.at[c], out_ref, o_send.at[c], o_recv, where)

    def give_final(c, i):
        mine = pl.ds(pl.multiple_of(c * rows, rows), rows)
        return copy(fin.at[i, mine], final_ref.at[i], f_send.at[c, i], f_recv.at[i], {"seq": c})

    def call_next():
        pl.semaphore_signal(go, inc=1, device_id={"seq": z + 1}, device_id_type=MESH)

    @pl.when(is_source)
    def _():
        pl.when(has_prev)(lambda: pl.semaphore_wait(go, 1))
        for i in range(2):
            give(i, server, 0).start()
        give(0, server, 0).wait_send()
        pl.when(has_next)(call_next)
        pl.when((z > 0) & jnp.logical_not(upper))(give_q.start)

    @pl.when(is_master)
    def _():
        for d, r in enumerate(twins):
            for i in range(2):
                give(i, {"inner": r}, d).start()
        pl.when(z > 0)(give_q.start)

    pl.when((z == 0) | is_master)(get_init.wait)

    @pl.when(z == 0)
    def _():
        get_q.wait()
        out_ref[...] = apply_net(q_v[...], *[state[i].astype(BF16) for i in range(3)])

    def sums(i):
        w = state[i]
        after = jnp.sum(w * w, axis=0, keepdims=True)
        scale = root[i] * lax.rsqrt(after + column_eps)
        total = after * (scale * scale) + column_eps
        root[i] = total * lax.rsqrt(total)
        return scale

    @pl.when(is_server)
    def _():
        @pl.loop(0, n)
        def _(c):
            @pl.when(c != sz)
            def _():
                for i in range(2):
                    take(c, x, i).wait_recv()
                    for d, r in enumerate(twins + [x]):
                        forward(c, i, r, d).start()

    @pl.when(is_source & upper)
    def _():
        pl.when(has_next)(lambda: pl.semaphore_wait(qgo, 1))
        give_q.start()

        @pl.when(has_prev)
        def _():
            pl.semaphore_signal(qgo, inc=1, device_id={"seq": z - 1}, device_id_type=MESH)

    @pl.when(is_master)
    def _():
        for i in range(3):
            w = state[i]
            root[i] = jnp.sqrt(jnp.sum(w * w, axis=0, keepdims=True) + column_eps)
        kv[mz, x, 1] = nv_v[...]
        get_key.wait()

        @pl.loop(0, n)
        def _(c):
            for r in range(m):
                for i in range(2):
                    pl.when((c != mz) | (r != x))(lambda: take(c, r, i).wait_recv())
            scales = [sums(i) for i in range(3)]
            ws = [state[i].astype(BF16) for i in range(3)]
            k = kv[c, :, 0].reshape(m * tok, head)
            nv = kv[c, :, 1].reshape(m * tok, head)
            for i, g in enumerate(span_grads(k, nv, ws, scales)):
                grad[i] = g
            for i in range(3):
                w = state[i] * scales[i]
                state[i] = w
                halves[c, i] = w.astype(BF16)
            ys = newton([grad[i] for i in range(3)])
            pl.when(c > 0)(lambda: give_half(c).start())
            for i in range(3):
                state[i] = state[i] + (step_size / half_root) * ys[i]

        for i in range(3):
            fin[i] = (state[i] * sums(i)).astype(BF16)

        @pl.loop(0, n)
        def _(d):
            c = n - 1 - d
            for i in range(3):
                pl.when(c != mz)(lambda: give_final(c, i).start())

        mine = pl.ds(pl.multiple_of(z * rows, rows), rows)
        final_ref[...] = fin[:, mine, :]

        @pl.loop(0, n)
        def _(c):
            for i in range(3):
                pl.when(c != mz)(lambda: give_final(c, i).wait_send())
            pl.when(c > 0)(lambda: give_half(c).wait_send())
        for d, r in enumerate(twins):
            for i in range(2):
                give(i, {"inner": r}, d).wait_send()

    @pl.when(is_server)
    def _():
        @pl.loop(1, n)
        def _(c):
            copy(queue.at[c], queue.at[c], q_send, q_recv.at[c], server).wait_recv()
            give_half(c).wait_recv()
            outs[c] = apply_net(queue[c], *[halves[c, i] for i in range(3)])
            give_out(c).start()

        @pl.loop(0, n)
        def _(c):
            pl.when(c > 0)(lambda: give_out(c).wait_send())

            @pl.when(c != sz)
            def _():
                for i in range(2):
                    for d, r in enumerate(twins + [x]):
                        forward(c, i, r, d).wait_send()

    @pl.when(is_source)
    def _():
        give(1, server, 0).wait_send()
        for i in range(3):
            give_final(0, i).wait_recv()

    @pl.when(z > 0)
    def _():
        give_q.wait_send()
        give_out(0).wait_recv()


def finish(out_ref, final_ref, out_hbm, final_hbm, wide, sem):
    first = pltpu.make_async_copy(out_ref, out_hbm, sem.at[0])
    first.start()
    wide[...] = final_ref[...].astype(F32)
    second = pltpu.make_async_copy(wide, final_hbm, sem.at[1])
    second.start()
    first.wait()
    second.wait()


def per_device(queries, keys, values, rates, video_start, span_len, init_weights):
    tok, head = queries.shape[1:]
    n, m, nb = lax.axis_size("seq"), lax.axis_size("inner"), lax.axis_size("batch")
    hidden = init_weights.shape[2]
    rows = init_weights.shape[1] // n
    vm = pl.BlockSpec(memory_space=pltpu.VMEM)
    hbm = pl.BlockSpec(memory_space=pl.ANY)
    dma = pltpu.SemaphoreType.DMA
    out, final = pl.pallas_call(
        functools.partial(kernel, n, m, nb),
        out_shape=(
            jax.ShapeDtypeStruct((tok, head), BF16),
            jax.ShapeDtypeStruct((3, rows, hidden), BF16),
        ),
        in_specs=[hbm] * 7,
        out_specs=(vm, vm),
        scratch_shapes=[
            pltpu.VMEM((n, m, 2, tok, head), BF16),
            pltpu.VMEM((n, tok, head), BF16),
            pltpu.VMEM((n, tok, head), BF16),
            pltpu.VMEM((n,) + init_weights.shape, BF16),
            pltpu.VMEM(init_weights.shape, F32),
            pltpu.VMEM((3, 1, hidden), F32),
            pltpu.VMEM(init_weights.shape, F32),
            pltpu.VMEM(init_weights.shape, BF16),
            pltpu.VMEM((tok, head), BF16),
            pltpu.VMEM((1, tok), F32),
            pltpu.VMEM((tok, head), BF16),
            pltpu.VMEM((tok, head), BF16),
            pltpu.VMEM((1, 1), jnp.int32),
            pltpu.VMEM((1, 1), jnp.int32),
            dma((7,)),
            dma((max(m - 1, 1), 2)),
            dma((n, m, 2)),
            dma((n, 2, m)),
            dma(()),
            dma((n,)),
            dma((n,)),
            dma((n,)),
            dma((n,)),
            dma(()),
            dma((n, 3)),
            dma((3,)),
            pltpu.SemaphoreType.REGULAR,
            pltpu.SemaphoreType.REGULAR,
        ],
        compiler_params=pltpu.CompilerParams(collective_id=0, has_side_effects=True),
    )(video_start[None], span_len, keys[0], values[0], rates, queries[0], init_weights)
    out, final = pl.pallas_call(
        finish,
        out_shape=(
            jax.ShapeDtypeStruct((tok, head), BF16),
            jax.ShapeDtypeStruct((3, rows, hidden), F32),
        ),
        in_specs=[vm, vm],
        out_specs=(hbm, hbm),
        scratch_shapes=[pltpu.VMEM((3, rows, hidden), F32), dma((2,))],
    )(out, final)
    return out[None], final[None]


def solution(mesh):
    in_specs = (
        P(("groups", "batch"), ("seq", "inner"), None),
        P(("groups", "batch"), ("seq", "inner"), None),
        P(("groups", "batch"), ("seq", "inner"), None),
        P(("groups", "batch"), ("seq", "inner")),
        P(("groups", "batch")),
        P(("groups", "batch"), "seq"),
        P(),
    )
    out_specs = (
        P(("groups", "batch"), ("seq", "inner"), None),
        P(("groups", "batch"), None, "seq", None),
    )
    return jax.shard_map(
        per_device, mesh=mesh, in_specs=in_specs, out_specs=out_specs, check_vma=False
    )
```

```python
import functools

import jax
import jax.numpy as jnp
from jax import lax
from jax.experimental import pallas as pl
from jax.experimental.pallas import tpu as pltpu
from jax.sharding import PartitionSpec as P

NS_STEPS = 5
CHUNKS = 2
CALL_AFTER = 1
MESH = pl.DeviceIdType.MESH
step_size = 0.1
norm_eps = 1e-07
column_eps = 1e-06
half_root = 0.5**0.5
F32, BF16 = jnp.float32, jnp.bfloat16


def dot(a, b, ca, cb):
    return lax.dot_general(a, b, (((ca,), (cb,)), ((), ())), preferred_element_type=F32)


def sigmoid(g):
    return 0.5 + 0.5 * jnp.tanh(0.5 * g)


def apply_net(rows, w1, w3, w2):
    gate = dot(rows, w1, 1, 0)
    up = dot(rows, w3, 1, 0)
    hidden = (gate * sigmoid(gate) * up).astype(BF16)
    return dot(hidden, w2, 1, 1).astype(BF16)


def span_grads(k, nv, ws, scales):
    gate = dot(k, ws[0], 1, 0) * scales[0]
    up = dot(k, ws[1], 1, 0) * scales[1]
    back = dot(nv, ws[2], 1, 0) * scales[2]
    s = sigmoid(gate)
    active = gate * s
    hidden = (active * up).astype(BF16)
    d_up = (back * active).astype(BF16)
    d_gate = (back * up * (s + active - active * s)).astype(BF16)
    return [dot(k, d_gate, 0, 0), dot(k, d_up, 0, 0), dot(nv, hidden, 0, 0)]


def newton(grads):
    size = grads[0].shape[0]
    at = [lax.broadcasted_iota(jnp.int32, (size, size), d) for d in range(2)]
    eye = jnp.where(at[0] == at[1], 1.5, 0.0).astype(F32)
    xs = [g.astype(BF16) for g in grads]
    scales = [
        half_root / (jnp.sqrt(jnp.sum(g * g, keepdims=True)) + norm_eps) for g in grads
    ]
    factors = [(dot(x, x, 1, 1) * (s * s) - eye).astype(BF16) for x, s in zip(xs, scales)]
    ys = [dot(f, x, 1, 0) * s for f, x, s in zip(factors, xs, scales)]
    for unused in range(1, NS_STEPS):
        xs = [y.astype(BF16) for y in ys]
        factors = [(dot(x, x, 1, 1) - eye).astype(BF16) for x in xs]
        ys = [dot(f, x, 1, 0) for f, x in zip(factors, xs)]
    sign = -1.0 if NS_STEPS % 2 == 0 else 1.0
    return ys if sign > 0 else [-y for y in ys]


def kernel(
    n, m, nb, start_ref, len_ref, key_ref, value_ref, rate_ref, q_ref, init_ref, out_ref, final_ref,
    kv, queue, outs, halves, state, root, grad, fin, val_v, rate_v, q_v, nv_v, first_v, len_v,
    in_sem, kv_send, kv_recv, pass_send, q_send, q_recv, h_send, h_recv, o_send, o_recv, f_send, f_recv,
    go, qgo,
):
    z, x, b = lax.axis_index("seq"), lax.axis_index("inner"), lax.axis_index("batch")
    tok, head = value_ref.shape
    rows = final_ref.shape[1]

    def home(v):
        return (n // 2) * (1 - lax.rem(v, 2))

    other = lax.rem(b + 1, nb)
    served = lax.rem(b + nb - 1, nb)
    mz, sz = home(b), home(served)
    is_master, is_server = z == mz, z == sz
    is_source = jnp.logical_not(is_master)
    upper = z > mz

    def same_side(lower):
        return (lower >= 0) & (lower + 1 < n) & ((lower + 1 < mz) | (lower > mz))

    has_next, has_prev = same_side(z), same_side(z - 1)
    twins = [lax.rem(x + d, m) for d in range(1, m)]

    barrier = pltpu.get_barrier_semaphore()

    def greet(where):
        pl.semaphore_signal(barrier, inc=1, device_id=where, device_id_type=MESH)

    @pl.when(is_master)
    def _():
        for r in twins:
            greet({"inner": r})
        for r in range(m):
            greet({"inner": r, "batch": other})

    @pl.when(is_server)
    def _():
        @pl.loop(0, n)
        def _(c):
            greet({"seq": c, "batch": served})

    pl.when(has_prev)(lambda: greet({"seq": z - 1}))

    def fetch(src, dst, i):
        return pltpu.make_async_copy(src, dst, in_sem.at[i])

    get_val = fetch(value_ref, val_v, 0)
    get_rate = fetch(rate_ref, rate_v, 1)
    get_q = fetch(q_ref, q_v, 2)
    get_init = fetch(init_ref, state, 3)
    get_key = fetch(key_ref, kv.at[mz, x, 0], 4)
    get_first = fetch(start_ref, first_v, 5)
    get_len = fetch(len_ref, len_v, 6)
    get_first.start()
    get_len.start()
    get_rate.start()
    get_val.start()
    pl.when(is_master)(get_key.start)
    pl.when(z == 0)(get_q.start)
    pl.when((z == 0) | is_master)(get_init.start)

    within = lax.broadcasted_iota(jnp.int32, (1, tok), 1) + x * tok
    position = within + z * (tok * m)
    eye = lax.broadcasted_iota(jnp.int32, (tok, tok), 0) == lax.broadcasted_iota(
        jnp.int32, (tok, tok), 1
    )
    get_first.wait()
    get_len.wait()
    get_rate.wait()
    valid = ((position >= first_v[0]) & (within < len_v[0, 0])).astype(F32)
    weight = rate_v[...] * valid
    column = jnp.sum(jnp.where(eye, weight, 0.0), axis=1, keepdims=True)
    get_val.wait()
    nv_v[...] = (-(column * val_v[...].astype(F32))).astype(BF16)

    pl.semaphore_wait(
        barrier,
        1
        + is_master.astype(jnp.int32) * (m - 1)
        + is_server.astype(jnp.int32) * m
        + has_next.astype(jnp.int32),
    )

    def copy(src, dst, send, recv, where):
        return pltpu.make_async_remote_copy(src, dst, send, recv, where, MESH)

    pieces = 2 * CHUNKS
    part = tok // CHUNKS

    def piece(c, r, j):
        return kv.at[c, r, j // CHUNKS, pl.ds(j % CHUNKS * part, part)]

    def give(j, where, slot):
        src = (key_ref if j < CHUNKS else nv_v).at[pl.ds(j % CHUNKS * part, part)]
        return copy(src, piece(z, x, j), kv_send.at[slot, j], kv_recv.at[z, x, j], where)

    def take(c, r, j):
        return copy(piece(c, r, j), piece(c, r, j), kv_send.at[0, j], kv_recv.at[c, r, j], {"seq": mz})

    def forward(c, j, r, slot):
        where = {"inner": r, "batch": served}
        block = piece(c, x, j)
        return copy(block, block, pass_send.at[c, j, slot], kv_recv.at[c, x, j], where)

    server = {"seq": mz, "batch": other}
    give_q = copy(q_ref, queue.at[z], q_send, q_recv.at[z], server)

    def give_half(c):
        return copy(halves.at[c], halves.at[c], h_send.at[c], h_recv.at[c], server)

    def give_out(c):
        where = {"seq": c, "batch": served}
        return copy(outs.at[c], out_ref, o_send.at[c], o_recv, where)

    def give_final(c, i):
        mine = pl.ds(pl.multiple_of(c * rows, rows), rows)
        return copy(fin.at[i, mine], final_ref.at[i], f_send.at[c, i], f_recv.at[i], {"seq": c})

    def call_next():
        pl.semaphore_signal(go, inc=1, device_id={"seq": z + 1}, device_id_type=MESH)

    @pl.when(is_source)
    def _():
        pl.when(has_prev)(lambda: pl.semaphore_wait(go, 1))
        for j in range(pieces):
            give(j, server, 0).start()
        for j in range(CALL_AFTER):
            give(j, server, 0).wait_send()
        pl.when(has_next)(call_next)
        pl.when((z > 0) & jnp.logical_not(upper))(give_q.start)

    @pl.when(is_master)
    def _():
        for d, r in enumerate(twins):
            for j in range(pieces):
                give(j, {"inner": r}, d).start()
        pl.when(z > 0)(give_q.start)

    pl.when((z == 0) | is_master)(get_init.wait)

    @pl.when(z == 0)
    def _():
        get_q.wait()
        out_ref[...] = apply_net(q_v[...], *[state[i].astype(BF16) for i in range(3)])

    def sums(i):
        w = state[i]
        after = jnp.sum(w * w, axis=0, keepdims=True)
        scale = root[i] * lax.rsqrt(after + column_eps)
        total = after * (scale * scale) + column_eps
        root[i] = total * lax.rsqrt(total)
        return scale

    @pl.when(is_server)
    def _():
        @pl.loop(0, n)
        def _(c):
            @pl.when(c != sz)
            def _():
                for j in range(pieces):
                    take(c, x, j).wait_recv()
                    for d, r in enumerate(twins + [x]):
                        forward(c, j, r, d).start()

    @pl.when(is_source & upper)
    def _():
        pl.when(has_next)(lambda: pl.semaphore_wait(qgo, 1))
        give_q.start()

        @pl.when(has_prev)
        def _():
            pl.semaphore_signal(qgo, inc=1, device_id={"seq": z - 1}, device_id_type=MESH)

    @pl.when(is_master)
    def _():
        for i in range(3):
            w = state[i]
            root[i] = jnp.sqrt(jnp.sum(w * w, axis=0, keepdims=True) + column_eps)
        kv[mz, x, 1] = nv_v[...]
        get_key.wait()

        @pl.loop(0, n)
        def _(c):
            for r in range(m):
                for j in range(pieces):
                    pl.when((c != mz) | (r != x))(lambda: take(c, r, j).wait_recv())
            scales = [sums(i) for i in range(3)]
            ws = [state[i].astype(BF16) for i in range(3)]
            k = kv[c, :, 0].reshape(m * tok, head)
            nv = kv[c, :, 1].reshape(m * tok, head)
            for i in range(3):
                w = state[i] * scales[i]
                state[i] = w
                halves[c, i] = w.astype(BF16)
            for i, g in enumerate(span_grads(k, nv, ws, scales)):
                grad[i] = g
            pl.when(c > 0)(lambda: give_half(c).start())
            ys = newton([grad[i] for i in range(3)])
            for i in range(3):
                state[i] = state[i] + (step_size / half_root) * ys[i]

        for i in range(3):
            fin[i] = (state[i] * sums(i)).astype(BF16)

        @pl.loop(0, n)
        def _(d):
            c = jnp.where(mz < n // 2, n - 1 - d, d)
            for i in range(3):
                pl.when(c != mz)(lambda: give_final(c, i).start())

        mine = pl.ds(pl.multiple_of(z * rows, rows), rows)
        final_ref[...] = fin[:, mine, :]

        @pl.loop(0, n)
        def _(c):
            for i in range(3):
                pl.when(c != mz)(lambda: give_final(c, i).wait_send())
            pl.when(c > 0)(lambda: give_half(c).wait_send())
        for d, r in enumerate(twins):
            for j in range(pieces):
                give(j, {"inner": r}, d).wait_send()

    @pl.when(is_server)
    def _():
        @pl.loop(1, n)
        def _(c):
            copy(queue.at[c], queue.at[c], q_send, q_recv.at[c], server).wait_recv()
            give_half(c).wait_recv()
            outs[c] = apply_net(queue[c], *[halves[c, i] for i in range(3)])
            give_out(c).start()

        @pl.loop(0, n)
        def _(c):
            pl.when(c > 0)(lambda: give_out(c).wait_send())

            @pl.when(c != sz)
            def _():
                for j in range(pieces):
                    for d, r in enumerate(twins + [x]):
                        forward(c, j, r, d).wait_send()

    @pl.when(is_source)
    def _():
        for j in range(CALL_AFTER, pieces):
            give(j, server, 0).wait_send()
        for i in range(3):
            give_final(0, i).wait_recv()

    @pl.when(z > 0)
    def _():
        give_q.wait_send()
        give_out(0).wait_recv()


def finish(out_ref, final_ref, out_hbm, final_hbm, wide, sem):
    first = pltpu.make_async_copy(out_ref, out_hbm, sem.at[0])
    first.start()
    wide[...] = final_ref[...].astype(F32)
    second = pltpu.make_async_copy(wide, final_hbm, sem.at[1])
    second.start()
    first.wait()
    second.wait()


def per_device(queries, keys, values, rates, video_start, span_len, init_weights):
    tok, head = queries.shape[1:]
    n, m, nb = lax.axis_size("seq"), lax.axis_size("inner"), lax.axis_size("batch")
    hidden = init_weights.shape[2]
    rows = init_weights.shape[1] // n
    vm = pl.BlockSpec(memory_space=pltpu.VMEM)
    hbm = pl.BlockSpec(memory_space=pl.ANY)
    dma = pltpu.SemaphoreType.DMA
    out, final = pl.pallas_call(
        functools.partial(kernel, n, m, nb),
        out_shape=(
            pltpu.VMEM((tok, head), BF16),
            pltpu.VMEM((3, rows, hidden), BF16),
        ),
        in_specs=[pl.BlockSpec(memory_space=pltpu.HBM)] * 7,
        out_specs=(vm, vm),
        scratch_shapes=[
            pltpu.VMEM((n, m, 2, tok, head), BF16),
            pltpu.VMEM((n, tok, head), BF16),
            pltpu.VMEM((n, tok, head), BF16),
            pltpu.VMEM((n,) + init_weights.shape, BF16),
            pltpu.VMEM(init_weights.shape, F32),
            pltpu.VMEM((3, 1, hidden), F32),
            pltpu.VMEM(init_weights.shape, F32),
            pltpu.VMEM(init_weights.shape, BF16),
            pltpu.VMEM((tok, head), BF16),
            pltpu.VMEM((1, tok), F32),
            pltpu.VMEM((tok, head), BF16),
            pltpu.VMEM((tok, head), BF16),
            pltpu.SMEM((1,), jnp.int32),
            pltpu.SMEM((1, 1), jnp.int32),
            dma((7,)),
            dma((max(m - 1, 1), 2 * CHUNKS)),
            dma((n, m, 2 * CHUNKS)),
            dma((n, 2 * CHUNKS, m)),
            dma(()),
            dma((n,)),
            dma((n,)),
            dma((n,)),
            dma((n,)),
            dma(()),
            dma((n, 3)),
            dma((3,)),
            pltpu.SemaphoreType.REGULAR,
            pltpu.SemaphoreType.REGULAR,
        ],
        compiler_params=pltpu.CompilerParams(collective_id=0, has_side_effects=True),
    )(video_start, span_len, keys[0], values[0], rates, queries[0], init_weights)
    out, final = pl.pallas_call(
        finish,
        out_shape=(
            jax.ShapeDtypeStruct((tok, head), BF16),
            jax.ShapeDtypeStruct((3, rows, hidden), F32),
        ),
        in_specs=[vm, vm],
        out_specs=(hbm, hbm),
        scratch_shapes=[pltpu.VMEM((3, rows, hidden), F32), dma((2,))],
    )(*[pltpu.with_memory_space_constraint(a, pltpu.VMEM) for a in (out, final)])
    return out[None], final[None]


def solution(mesh):
    in_specs = (
        P(("groups", "batch"), ("seq", "inner"), None),
        P(("groups", "batch"), ("seq", "inner"), None),
        P(("groups", "batch"), ("seq", "inner"), None),
        P(("groups", "batch"), ("seq", "inner")),
        P(("groups", "batch")),
        P(("groups", "batch"), "seq"),
        P(),
    )
    out_specs = (
        P(("groups", "batch"), ("seq", "inner"), None),
        P(("groups", "batch"), None, "seq", None),
    )
    return jax.shard_map(
        per_device, mesh=mesh, in_specs=in_specs, out_specs=out_specs, check_vma=False
    )
```

```python
import functools

import jax
import jax.numpy as jnp
from jax import lax
from jax.experimental import pallas as pl
from jax.experimental.pallas import tpu as pltpu
from jax.sharding import PartitionSpec as P

NS_STEPS = 5
CHUNKS = 2
CALL_AFTER = 1
QUERY_AFTER = 2
MESH = pl.DeviceIdType.MESH
step_size = 0.1
norm_eps = 1e-07
column_eps = 1e-06
half_root = 0.5**0.5
F32, BF16 = jnp.float32, jnp.bfloat16


def dot(a, b, ca, cb):
    return lax.dot_general(a, b, (((ca,), (cb,)), ((), ())), preferred_element_type=F32)


def sigmoid(g):
    return 0.5 + 0.5 * jnp.tanh(0.5 * g)


def apply_net(rows, w1, w3, w2):
    gate = dot(rows, w1, 1, 0)
    up = dot(rows, w3, 1, 0)
    hidden = (gate * sigmoid(gate) * up).astype(BF16)
    return dot(hidden, w2, 1, 1).astype(BF16)


def span_grads(k, nv, ws, scales):
    gate = dot(k, ws[0], 1, 0) * scales[0]
    up = dot(k, ws[1], 1, 0) * scales[1]
    back = dot(nv, ws[2], 1, 0) * scales[2]
    s = sigmoid(gate)
    active = gate * s
    hidden = (active * up).astype(BF16)
    d_up = (back * active).astype(BF16)
    d_gate = (back * up * (s + active - active * s)).astype(BF16)
    return [dot(k, d_gate, 0, 0), dot(k, d_up, 0, 0), dot(nv, hidden, 0, 0)]


def newton(grads):
    size = grads[0].shape[0]
    at = [lax.broadcasted_iota(jnp.int32, (size, size), d) for d in range(2)]
    eye = jnp.where(at[0] == at[1], 1.5, 0.0).astype(F32)
    xs = [g.astype(BF16) for g in grads]
    scales = [
        half_root / (jnp.sqrt(jnp.sum(g * g, keepdims=True)) + norm_eps) for g in grads
    ]
    factors = [(dot(x, x, 1, 1) * (s * s) - eye).astype(BF16) for x, s in zip(xs, scales)]
    ys = [dot(f, x, 1, 0) * s for f, x, s in zip(factors, xs, scales)]
    for unused in range(1, NS_STEPS):
        xs = [y.astype(BF16) for y in ys]
        factors = [(dot(x, x, 1, 1) - eye).astype(BF16) for x in xs]
        ys = [dot(f, x, 1, 0) for f, x in zip(factors, xs)]
    sign = -1.0 if NS_STEPS % 2 == 0 else 1.0
    return ys if sign > 0 else [-y for y in ys]


def kernel(
    n, m, nb, start_ref, len_ref, key_ref, value_ref, rate_ref, q_ref, init_ref, out_ref, final_ref,
    kv, queue, outs, halves, state, root, grad, fin, val_v, rate_v, q_v, nv_v,
    in_sem, kv_send, twin_send, part_recv, kv_recv, pass_send, q_send, q_recv, h_send, h_recv, o_send, o_recv, f_send, f_recv,
    go, qgo,
):
    z, x, b = lax.axis_index("seq"), lax.axis_index("inner"), lax.axis_index("batch")
    tok, head = value_ref.shape
    rows = final_ref.shape[1]

    def home(v):
        return (n // 2) * (1 - lax.rem(v, 2))

    other = lax.rem(b + 1, nb)
    served = lax.rem(b + nb - 1, nb)
    mz, sz = home(b), home(served)
    is_master, is_server = z == mz, z == sz
    is_source = jnp.logical_not(is_master)
    upper = z > mz

    def same_side(lower):
        return (lower >= 0) & (lower + 1 < n) & ((lower + 1 < mz) | (lower > mz))

    has_next, has_prev = same_side(z), same_side(z - 1)
    twins = [lax.rem(x + d, m) for d in range(1, m)]

    barrier = pltpu.get_barrier_semaphore()

    def greet(where):
        pl.semaphore_signal(barrier, inc=1, device_id=where, device_id_type=MESH)

    @pl.when(is_master)
    def _():
        for r in twins:
            greet({"inner": r})
        for r in range(m):
            greet({"inner": r, "batch": other})

    @pl.when(is_server)
    def _():
        @pl.loop(0, n)
        def _(c):
            greet({"seq": c, "batch": served})

    pl.when(has_prev)(lambda: greet({"seq": z - 1}))
    many = mz + 2 < n
    is_first, is_last = upper & many & (z == mz + 1), upper & many & (z == n - 1)
    holds_last = upper & many & (z == n - 2)
    pl.when(is_first)(lambda: greet({"seq": n - 1}))

    def fetch(src, dst, i):
        return pltpu.make_async_copy(src, dst, in_sem.at[i])

    get_val = fetch(value_ref, val_v, 0)
    get_rate = fetch(rate_ref, rate_v, 1)
    get_q = fetch(q_ref, q_v, 2)
    get_init = fetch(init_ref, state, 3)
    get_key = fetch(key_ref, kv.at[mz, x, 0], 4)
    get_rate.start()
    get_val.start()
    pl.when(is_master)(get_key.start)
    pl.when(z == 0)(get_q.start)
    pl.when((z == 0) | is_master)(get_init.start)

    within = lax.broadcasted_iota(jnp.int32, (1, tok), 1) + x * tok
    position = within + z * (tok * m)
    eye = lax.broadcasted_iota(jnp.int32, (tok, tok), 0) == lax.broadcasted_iota(
        jnp.int32, (tok, tok), 1
    )
    get_rate.wait()
    valid = ((position >= start_ref[0]) & (within < len_ref[0, 0])).astype(F32)
    weight = rate_v[...] * valid
    column = jnp.sum(jnp.where(eye, weight, 0.0), axis=1, keepdims=True)
    get_val.wait()
    nv_v[...] = (-(column * val_v[...].astype(F32))).astype(BF16)

    pl.semaphore_wait(
        barrier,
        1
        + is_master.astype(jnp.int32) * (m - 1)
        + is_server.astype(jnp.int32) * m
        + has_next.astype(jnp.int32)
        + is_last.astype(jnp.int32),
    )

    def copy(src, dst, send, recv, where):
        return pltpu.make_async_remote_copy(src, dst, send, recv, where, MESH)

    pieces = 2 * CHUNKS
    part = tok // CHUNKS

    def piece(c, r, j):
        return kv.at[c, r, j // CHUNKS, pl.ds(j % CHUNKS * part, part)]

    def own_piece(j):
        return (key_ref if j < CHUNKS else nv_v).at[pl.ds(j % CHUNKS * part, part)]

    def give(j):
        send = kv_send.at[min(j, CHUNKS)]
        return copy(own_piece(j), piece(z, x, j), send, part_recv.at[z, j], server)

    def sent(j):
        return give(j) if j < CHUNKS else copy(nv_v, nv_v, kv_send.at[j], part_recv.at[z, j], server)

    def give_twin(j, d):
        where = {"inner": twins[d]}
        return copy(own_piece(j), piece(z, x, j), twin_send.at[d], kv_recv.at[z, x], where)

    def take_piece(c, j):
        return copy(piece(c, x, j), piece(c, x, j), pass_send, part_recv.at[c, j], server)

    def take(c, r, send=None):
        block = kv.at[c, r]
        return copy(block, block, twin_send.at[0] if send is None else send, kv_recv.at[c, r], server)

    def forward(c, j, r):
        where = {"inner": r, "batch": served}
        block = piece(c, x, j)
        return copy(block, block, pass_send, kv_recv.at[c, x], where)

    server = {"seq": mz, "batch": other}

    def give_query(h):
        half = pl.ds(h * (tok // 2), tok // 2)
        return copy(q_ref.at[half], queue.at[z, half], q_send.at[h], q_recv.at[z], server)

    def give_queries():
        for h in range(2):
            give_query(h).start()

    def give_half(c):
        return copy(halves.at[c], halves.at[c], h_send, h_recv.at[c], server)

    def give_out(c):
        where = {"seq": c, "batch": served}
        return copy(outs.at[c], out_ref, o_send, o_recv, where)

    def give_final(c, i):
        mine = pl.ds(pl.multiple_of(c * rows, rows), rows)
        return copy(fin.at[i, mine], final_ref.at[i], f_send, f_recv, {"seq": c})

    def call_next():
        pl.semaphore_signal(go, inc=1, device_id={"seq": z + 1}, device_id_type=MESH)

    @pl.when(is_source)
    def _():
        pl.when(has_prev)(lambda: pl.semaphore_wait(go, 1))
        for j in range(pieces):
            give(j).start()
        for j in range(CALL_AFTER):
            sent(j).wait_send()
        pl.when(has_next)(call_next)
        pl.when((z > 0) & jnp.logical_not(upper))(give_queries)

    @pl.when(is_master)
    def _():
        for d, r in enumerate(twins):
            for j in range(pieces):
                give_twin(j, d).start()
        pl.when(z > 0)(give_queries)

    pl.when((z == 0) | is_master)(get_init.wait)

    @pl.when(z == 0)
    def _():
        get_q.wait()
        out_ref[...] = apply_net(q_v[...], *[state[i].astype(BF16) for i in range(3)])

    def sums(i):
        w = state[i]
        after = jnp.sum(w * w, axis=0, keepdims=True)
        scale = root[i] * lax.rsqrt(after + column_eps)
        total = after * (scale * scale) + column_eps
        root[i] = total * lax.rsqrt(total)
        return scale

    @pl.when(is_server)
    def _():
        @pl.loop(0, n)
        def _(c):
            @pl.when(c != sz)
            def _():
                for j in range(pieces):
                    take_piece(c, j).wait_recv()
                    for r in twins + [x]:
                        forward(c, j, r).start()

    def call_query(where):
        pl.semaphore_signal(qgo, inc=1, device_id={"seq": where}, device_id_type=MESH)

    @pl.when(is_source & upper)
    def _():
        @pl.when(is_last)
        def _():
            for j in range(CALL_AFTER, QUERY_AFTER):
                sent(j).wait_send()
            call_query(mz + 1)

        pl.when(many)(lambda: pl.semaphore_wait(qgo, 1))
        give_queries()
        pl.when(holds_last)(lambda: give_query(0).wait_send())
        pl.when(has_next)(lambda: call_query(z + 1))

    @pl.when(is_master)
    def _():
        for i in range(3):
            w = state[i]
            root[i] = jnp.sqrt(jnp.sum(w * w, axis=0, keepdims=True) + column_eps)
        kv[mz, x, 1] = nv_v[...]
        get_key.wait()

        def train(c, last):
            for d in range(m):
                r = lax.rem(x + d, m)
                pl.when((c != mz) | (r != x))(lambda: take(c, r).wait_recv())
            scales = [sums(i) for i in range(3)]
            ws = [state[i].astype(BF16) for i in range(3)]
            for i in range(3):
                w = state[i] * scales[i]
                state[i] = w
                halves[c, i] = w.astype(BF16)
            k = kv[c, :, 0].reshape(m * tok, head)
            nv = kv[c, :, 1].reshape(m * tok, head)
            grads = span_grads(k, nv, ws, scales)
            if last:
                for i in range(3):
                    grad[i] = grads[i]
                give_half(c).start()
                grads = [grad[i] for i in range(3)]
            for i, y in enumerate(newton(grads)):
                state[i] = state[i] + (step_size / half_root) * y
            if not last:
                pl.when(c > 0)(lambda: give_half(c).start())

        pl.loop(0, n - 1)(lambda c: train(c, False))
        train(n - 1, True)

        far = jnp.where(mz < n // 2, n - 1, 0)
        for i in range(3):
            fin[i] = (state[i] * sums(i)).astype(BF16)
            give_final(far, i).start()

        @pl.loop(1, n)
        def _(d):
            c = jnp.where(mz < n // 2, n - 1 - d, d)
            for i in range(3):
                pl.when(c != mz)(lambda: give_final(c, i).start())

        mine = pl.ds(pl.multiple_of(z * rows, rows), rows)
        final_ref[...] = fin[:, mine, :]

        rest = fin.at[:, pl.ds(0, (n - 1) * rows)]
        copy(rest, rest, f_send, f_recv, server).wait_send()
        rest = halves.at[pl.ds(1, n - 1)]
        copy(rest, rest, h_send, h_recv.at[0], server).wait_send()
        for d, r in enumerate(twins):
            take(z, x, twin_send.at[d]).wait_send()

    @pl.when(is_server)
    def _():
        @pl.loop(1, n)
        def _(c):
            copy(queue.at[c], queue.at[c], q_send.at[0], q_recv.at[c], server).wait_recv()
            give_half(c).wait_recv()
            outs[c] = apply_net(queue[c], *[halves[c, i] for i in range(3)])
            give_out(c).start()

        rest = outs.at[pl.ds(1, n - 1)]
        copy(rest, rest, o_send, o_recv, server).wait_send()
        rest = kv.at[pl.ds(0, n - 1)]
        copy(rest, rest, pass_send, kv_recv.at[0, 0], server).wait_send()

    @pl.when(is_source)
    def _():
        for j in range(CALL_AFTER, QUERY_AFTER):
            pl.when(jnp.logical_not(is_last))(sent(j).wait_send)
        for j in range(QUERY_AFTER, CHUNKS + 1):
            sent(j).wait_send()
        copy(final_ref, final_ref, f_send, f_recv, {"seq": 0}).wait_recv()

    @pl.when(z > 0)
    def _():
        pl.when(jnp.logical_not(holds_last))(lambda: give_query(0).wait_send())
        give_query(1).wait_send()
        give_out(0).wait_recv()


def finish(out_ref, final_ref, out_hbm, final_hbm, wide, sem):
    first = pltpu.make_async_copy(out_ref, out_hbm, sem.at[0])
    first.start()
    wide[...] = final_ref[...].astype(F32)
    second = pltpu.make_async_copy(wide, final_hbm, sem.at[1])
    second.start()
    first.wait()
    second.wait()


def per_device(queries, keys, values, rates, video_start, span_len, init_weights):
    tok, head = queries.shape[1:]
    n, m, nb = lax.axis_size("seq"), lax.axis_size("inner"), lax.axis_size("batch")
    hidden = init_weights.shape[2]
    rows = init_weights.shape[1] // n
    vm = pl.BlockSpec(memory_space=pltpu.VMEM)
    hbm = pl.BlockSpec(memory_space=pl.ANY)
    dma = pltpu.SemaphoreType.DMA
    out, final = pl.pallas_call(
        functools.partial(kernel, n, m, nb),
        out_shape=(
            pltpu.VMEM((tok, head), BF16),
            pltpu.VMEM((3, rows, hidden), BF16),
        ),
        in_specs=[pl.BlockSpec(memory_space=pltpu.SMEM)] * 2 + [hbm] * 5,
        out_specs=(vm, vm),
        scratch_shapes=[
            pltpu.VMEM((n, m, 2, tok, head), BF16),
            pltpu.VMEM((n, tok, head), BF16),
            pltpu.VMEM((n, tok, head), BF16),
            pltpu.VMEM((n,) + init_weights.shape, BF16),
            pltpu.VMEM(init_weights.shape, F32),
            pltpu.VMEM((3, 1, hidden), F32),
            pltpu.VMEM(init_weights.shape, F32),
            pltpu.VMEM(init_weights.shape, BF16),
            pltpu.VMEM((tok, head), BF16),
            pltpu.VMEM((1, tok), F32),
            pltpu.VMEM((tok, head), BF16),
            pltpu.VMEM((tok, head), BF16),
            dma((5,)),
            dma((CHUNKS + 1,)),
            dma((max(m - 1, 1),)),
            dma((n, 2 * CHUNKS)),
            dma((n, m)),
            dma(()),
            dma((2,)),
            dma((n,)),
            dma(()),
            dma((n,)),
            dma(()),
            dma(()),
            dma(()),
            dma(()),
            pltpu.SemaphoreType.REGULAR,
            pltpu.SemaphoreType.REGULAR,
        ],
        compiler_params=pltpu.CompilerParams(collective_id=0, has_side_effects=True),
    )(video_start, span_len, keys[0], values[0], rates, queries[0], init_weights)
    out, final = pl.pallas_call(
        finish,
        out_shape=(
            jax.ShapeDtypeStruct((tok, head), BF16),
            jax.ShapeDtypeStruct((3, rows, hidden), F32),
        ),
        in_specs=[vm, vm],
        out_specs=(hbm, hbm),
        scratch_shapes=[pltpu.VMEM((3, rows, hidden), F32), dma((2,))],
    )(*[pltpu.with_memory_space_constraint(a, pltpu.VMEM) for a in (out, final)])
    return out[None], final[None]


def solution(mesh):
    in_specs = (
        P(("groups", "batch"), ("seq", "inner"), None),
        P(("groups", "batch"), ("seq", "inner"), None),
        P(("groups", "batch"), ("seq", "inner"), None),
        P(("groups", "batch"), ("seq", "inner")),
        P(("groups", "batch")),
        P(("groups", "batch"), "seq"),
        P(),
    )
    out_specs = (
        P(("groups", "batch"), ("seq", "inner"), None),
        P(("groups", "batch"), None, "seq", None),
    )
    return jax.shard_map(
        per_device, mesh=mesh, in_specs=in_specs, out_specs=out_specs, check_vma=False
    )
```

```python
import functools

import jax
import jax.numpy as jnp
from jax import lax
from jax.experimental import pallas as pl
from jax.experimental.pallas import tpu as pltpu
from jax.sharding import PartitionSpec as P

NS_STEPS = 5
CHUNKS = 2
CALL_AFTER = 1
QUERY_AFTER = 2
MESH = pl.DeviceIdType.MESH
step_size = 0.1
norm_eps = 1e-07
column_eps = 1e-06
half_root = 0.5**0.5
F32, BF16 = jnp.float32, jnp.bfloat16


def dot(a, b, ca, cb):
    return lax.dot_general(a, b, (((ca,), (cb,)), ((), ())), preferred_element_type=F32)


def sigmoid(g):
    return 0.5 + 0.5 * jnp.tanh(0.5 * g)


def apply_net(rows, w1, w3, w2):
    gate = dot(rows, w1, 1, 0)
    up = dot(rows, w3, 1, 0)
    hidden = (gate * sigmoid(gate) * up).astype(BF16)
    return dot(hidden, w2, 1, 1).astype(BF16)


def span_grads(k, nv, ws, scales):
    gate = dot(k, ws[0], 1, 0) * scales[0]
    up = dot(k, ws[1], 1, 0) * scales[1]
    back = dot(nv, ws[2], 1, 0) * scales[2]
    s = sigmoid(gate)
    active = gate * s
    hidden = (active * up).astype(BF16)
    d_up = (back * active).astype(BF16)
    d_gate = (back * up * (s + active - active * s)).astype(BF16)
    return [dot(k, d_gate, 0, 0), dot(k, d_up, 0, 0), dot(nv, hidden, 0, 0)]


def newton(grads):
    size = grads[0].shape[0]
    at = [lax.broadcasted_iota(jnp.int32, (size, size), d) for d in range(2)]
    eye = jnp.where(at[0] == at[1], 1.5, 0.0).astype(F32)
    xs = [g.astype(BF16) for g in grads]
    scales = [
        half_root / (jnp.sqrt(jnp.sum(g * g, keepdims=True)) + norm_eps) for g in grads
    ]
    factors = [(dot(x, x, 1, 1) * (s * s) - eye).astype(BF16) for x, s in zip(xs, scales)]
    ys = [dot(f, x, 1, 0) * s for f, x, s in zip(factors, xs, scales)]
    for unused in range(1, NS_STEPS):
        xs = [y.astype(BF16) for y in ys]
        factors = [(dot(x, x, 1, 1) - eye).astype(BF16) for x in xs]
        ys = [dot(f, x, 1, 0) for f, x in zip(factors, xs)]
    sign = -1.0 if NS_STEPS % 2 == 0 else 1.0
    return ys if sign > 0 else [-y for y in ys]


def kernel(
    n, m, nb, start_ref, len_ref, key_ref, value_ref, rate_ref, q_ref, init_ref, out_ref, final_ref,
    kv, queue, outs, halves, state, root, grad, fin, val_v, rate_v, q_v, nv_v,
    in_sem, kv_send, twin_send, part_recv, kv_recv, pass_send, q_send, q_recv, h_send, h_recv, o_send, o_recv, f_send, f_recv,
    go, qgo,
):
    z, x, b = lax.axis_index("seq"), lax.axis_index("inner"), lax.axis_index("batch")
    tok, head = value_ref.shape
    rows = final_ref.shape[1]

    def home(v):
        return (n // 2) * (1 - lax.rem(v, 2))

    other = lax.rem(b + 1, nb)
    served = lax.rem(b + nb - 1, nb)
    mz, sz = home(b), home(served)
    is_master, is_server = z == mz, z == sz
    is_source = jnp.logical_not(is_master)
    upper = z > mz

    def same_side(lower):
        return (lower >= 0) & (lower + 1 < n) & ((lower + 1 < mz) | (lower > mz))

    has_next, has_prev = same_side(z), same_side(z - 1)
    twins = [lax.rem(x + d, m) for d in range(1, m)]

    barrier = pltpu.get_barrier_semaphore()

    def greet(where):
        pl.semaphore_signal(barrier, inc=1, device_id=where, device_id_type=MESH)

    @pl.when(is_master)
    def _():
        for r in twins:
            greet({"inner": r})
        for r in range(m):
            greet({"inner": r, "batch": other})

    @pl.when(is_server)
    def _():
        @pl.loop(0, n)
        def _(c):
            greet({"seq": c, "batch": served})

    pl.when(has_prev)(lambda: greet({"seq": z - 1}))
    many = mz + 2 < n
    is_first, is_last = upper & many & (z == mz + 1), upper & many & (z == n - 1)
    holds_last = upper & many & (z == n - 2)
    pl.when(is_first)(lambda: greet({"seq": n - 1}))

    def fetch(src, dst, i):
        return pltpu.make_async_copy(src, dst, in_sem.at[i])

    get_val = fetch(value_ref, val_v, 0)
    get_rate = fetch(rate_ref, rate_v, 1)
    get_q = fetch(q_ref, q_v, 2)
    get_init = fetch(init_ref, state, 3)
    get_key = fetch(key_ref, kv.at[mz, x, 0], 4)
    get_rate.start()
    get_val.start()
    pl.when(is_master)(get_key.start)
    pl.when(z == 0)(get_q.start)
    pl.when((z == 0) | is_master)(get_init.start)

    pl.semaphore_wait(
        barrier,
        1
        + is_master.astype(jnp.int32) * (m - 1)
        + is_server.astype(jnp.int32) * m
        + has_next.astype(jnp.int32)
        + is_last.astype(jnp.int32),
    )

    def copy(src, dst, send, recv, where):
        return pltpu.make_async_remote_copy(src, dst, send, recv, where, MESH)

    pieces = 2 * CHUNKS
    part = tok // CHUNKS

    def piece(c, r, j):
        return kv.at[c, r, j // CHUNKS, pl.ds(j % CHUNKS * part, part)]

    def own_piece(j):
        return (key_ref if j < CHUNKS else nv_v).at[pl.ds(j % CHUNKS * part, part)]

    def give(j):
        send = kv_send.at[min(j, CHUNKS)]
        return copy(own_piece(j), piece(z, x, j), send, part_recv.at[z, j], server)

    def sent(j):
        return give(j) if j < CHUNKS else copy(nv_v, nv_v, kv_send.at[j], part_recv.at[z, j], server)

    def give_twin(j, d):
        where = {"inner": twins[d]}
        return copy(own_piece(j), piece(z, x, j), twin_send.at[d], kv_recv.at[z, x], where)

    def take_piece(c, j):
        return copy(piece(c, x, j), piece(c, x, j), pass_send, part_recv.at[c, j], server)

    def take(c, r, send=None):
        block = kv.at[c, r]
        return copy(block, block, twin_send.at[0] if send is None else send, kv_recv.at[c, r], server)

    def forward(c, j, r):
        where = {"inner": r, "batch": served}
        block = piece(c, x, j)
        return copy(block, block, pass_send, kv_recv.at[c, x], where)

    server = {"seq": mz, "batch": other}

    def give_query(h):
        half = pl.ds(h * (tok // 2), tok // 2)
        return copy(q_ref.at[half], queue.at[z, half], q_send.at[h], q_recv.at[z], server)

    def give_queries():
        for h in range(2):
            give_query(h).start()

    def give_half(c):
        return copy(halves.at[c], halves.at[c], h_send, h_recv.at[c], server)

    def give_out(c):
        where = {"seq": c, "batch": served}
        return copy(outs.at[c], out_ref, o_send, o_recv, where)

    def give_final(c, i):
        mine = pl.ds(pl.multiple_of(c * rows, rows), rows)
        return copy(fin.at[i, mine], final_ref.at[i], f_send, f_recv, {"seq": c})

    def call_next():
        pl.semaphore_signal(go, inc=1, device_id={"seq": z + 1}, device_id_type=MESH)

    @pl.when(is_source)
    def _():
        pl.when(has_prev)(lambda: pl.semaphore_wait(go, 1))
        for j in range(CHUNKS):
            give(j).start()

    @pl.when(is_master)
    def _():
        for d, r in enumerate(twins):
            for j in range(CHUNKS):
                give_twin(j, d).start()

    within = lax.broadcasted_iota(jnp.int32, (1, tok), 1) + x * tok
    position = within + z * (tok * m)
    eye = lax.broadcasted_iota(jnp.int32, (tok, tok), 0) == lax.broadcasted_iota(
        jnp.int32, (tok, tok), 1
    )
    get_rate.wait()
    valid = ((position >= start_ref[0]) & (within < len_ref[0, 0])).astype(F32)
    weight = rate_v[...] * valid
    column = jnp.sum(jnp.where(eye, weight, 0.0), axis=1, keepdims=True)
    get_val.wait()
    nv_v[...] = (-(column * val_v[...].astype(F32))).astype(BF16)

    @pl.when(is_source)
    def _():
        for j in range(CHUNKS, pieces):
            give(j).start()
        for j in range(CALL_AFTER):
            sent(j).wait_send()
        pl.when(has_next)(call_next)
        pl.when((z > 0) & jnp.logical_not(upper))(give_queries)

    @pl.when(is_master)
    def _():
        for d, r in enumerate(twins):
            for j in range(CHUNKS, pieces):
                give_twin(j, d).start()
        pl.when(z > 0)(give_queries)

    pl.when((z == 0) | is_master)(get_init.wait)

    @pl.when(z == 0)
    def _():
        get_q.wait()
        out_ref[...] = apply_net(q_v[...], *[state[i].astype(BF16) for i in range(3)])

    def sums(i):
        w = state[i]
        after = jnp.sum(w * w, axis=0, keepdims=True)
        scale = root[i] * lax.rsqrt(after + column_eps)
        total = after * (scale * scale) + column_eps
        root[i] = total * lax.rsqrt(total)
        return scale

    @pl.when(is_server)
    def _():
        @pl.loop(0, n)
        def _(c):
            @pl.when(c != sz)
            def _():
                for j in range(pieces):
                    take_piece(c, j).wait_recv()
                    for r in twins + [x]:
                        forward(c, j, r).start()

    def call_query(where):
        pl.semaphore_signal(qgo, inc=1, device_id={"seq": where}, device_id_type=MESH)

    @pl.when(is_source & upper)
    def _():
        @pl.when(is_last)
        def _():
            for j in range(CALL_AFTER, QUERY_AFTER):
                sent(j).wait_send()
            call_query(mz + 1)

        pl.when(many)(lambda: pl.semaphore_wait(qgo, 1))
        give_queries()
        pl.when(holds_last)(lambda: give_query(0).wait_send())
        pl.when(has_next)(lambda: call_query(z + 1))

    @pl.when(is_master)
    def _():
        for i in range(3):
            w = state[i]
            root[i] = jnp.sqrt(jnp.sum(w * w, axis=0, keepdims=True) + column_eps)
        kv[mz, x, 1] = nv_v[...]
        get_key.wait()

        def train(c, split=False, last=False):
            def await_block(r):
                pl.when((c != mz) | (r != x))(lambda: take(c, r).wait_recv())

            await_block(x)
            if not split:
                for r in twins:
                    await_block(r)
            scales = [sums(i) for i in range(3)]
            ws = [state[i].astype(BF16) for i in range(3)]
            if split:
                for d, r in enumerate([x] + twins):
                    if d > 0:
                        await_block(r)
                    grads = span_grads(kv[c, r, 0], kv[c, r, 1], ws, scales)
                    if d > 0:
                        grads = [grad[i] + grads[i] for i in range(3)]
                    if d < m - 1:
                        for i in range(3):
                            grad[i] = grads[i]
            for i in range(3):
                w = state[i] * scales[i]
                state[i] = w
                halves[c, i] = w.astype(BF16)
            if not split:
                k = kv[c, :, 0].reshape(m * tok, head)
                nv = kv[c, :, 1].reshape(m * tok, head)
                grads = span_grads(k, nv, ws, scales)
            if last:
                for i in range(3):
                    grad[i] = grads[i]
                give_half(c).start()
                grads = [grad[i] for i in range(3)]
            for i, y in enumerate(newton(grads)):
                state[i] = state[i] + (step_size / half_root) * y
            if not last:
                pl.when(c > 0)(lambda: give_half(c).start())

        pl.loop(0, 2)(lambda c: train(c, split=True))
        pl.loop(2, n - 1)(train)
        train(n - 1, last=True)

        far = jnp.where(mz < n // 2, n - 1, 0)
        for i in range(3):
            fin[i] = (state[i] * sums(i)).astype(BF16)
            give_final(far, i).start()

        @pl.loop(1, n)
        def _(d):
            c = jnp.where(mz < n // 2, n - 1 - d, d)
            for i in range(3):
                pl.when(c != mz)(lambda: give_final(c, i).start())

        mine = pl.ds(pl.multiple_of(z * rows, rows), rows)
        final_ref[...] = fin[:, mine, :]

        rest = fin.at[:, pl.ds(0, (n - 1) * rows)]
        copy(rest, rest, f_send, f_recv, server).wait_send()
        rest = halves.at[pl.ds(1, n - 1)]
        copy(rest, rest, h_send, h_recv.at[0], server).wait_send()
        for d, r in enumerate(twins):
            take(z, x, twin_send.at[d]).wait_send()

    @pl.when(is_server)
    def _():
        @pl.loop(1, n)
        def _(c):
            copy(queue.at[c], queue.at[c], q_send.at[0], q_recv.at[c], server).wait_recv()
            give_half(c).wait_recv()
            outs[c] = apply_net(queue[c], *[halves[c, i] for i in range(3)])
            give_out(c).start()

        rest = outs.at[pl.ds(1, n - 1)]
        copy(rest, rest, o_send, o_recv, server).wait_send()
        rest = kv.at[pl.ds(0, n - 1)]
        copy(rest, rest, pass_send, kv_recv.at[0, 0], server).wait_send()

    @pl.when(is_source)
    def _():
        for j in range(CALL_AFTER, QUERY_AFTER):
            pl.when(jnp.logical_not(is_last))(sent(j).wait_send)
        for j in range(QUERY_AFTER, CHUNKS + 1):
            sent(j).wait_send()
        copy(final_ref, final_ref, f_send, f_recv, {"seq": 0}).wait_recv()

    @pl.when(z > 0)
    def _():
        pl.when(jnp.logical_not(holds_last))(lambda: give_query(0).wait_send())
        give_query(1).wait_send()
        give_out(0).wait_recv()


def finish(out_ref, final_ref, out_hbm, final_hbm, wide, sem):
    first = pltpu.make_async_copy(out_ref, out_hbm, sem.at[0])
    first.start()
    wide[...] = final_ref[...].astype(F32)
    second = pltpu.make_async_copy(wide, final_hbm, sem.at[1])
    second.start()
    first.wait()
    second.wait()


def per_device(queries, keys, values, rates, video_start, span_len, init_weights):
    tok, head = queries.shape[1:]
    n, m, nb = lax.axis_size("seq"), lax.axis_size("inner"), lax.axis_size("batch")
    hidden = init_weights.shape[2]
    rows = init_weights.shape[1] // n
    vm = pl.BlockSpec(memory_space=pltpu.VMEM)
    hbm = pl.BlockSpec(memory_space=pl.ANY)
    dma = pltpu.SemaphoreType.DMA
    out, final = pl.pallas_call(
        functools.partial(kernel, n, m, nb),
        out_shape=(
            pltpu.VMEM((tok, head), BF16),
            pltpu.VMEM((3, rows, hidden), BF16),
        ),
        in_specs=[pl.BlockSpec(memory_space=pltpu.SMEM)] * 2 + [hbm] * 5,
        out_specs=(vm, vm),
        scratch_shapes=[
            pltpu.VMEM((n, m, 2, tok, head), BF16),
            pltpu.VMEM((n, tok, head), BF16),
            pltpu.VMEM((n, tok, head), BF16),
            pltpu.VMEM((n,) + init_weights.shape, BF16),
            pltpu.VMEM(init_weights.shape, F32),
            pltpu.VMEM((3, 1, hidden), F32),
            pltpu.VMEM(init_weights.shape, F32),
            pltpu.VMEM(init_weights.shape, BF16),
            pltpu.VMEM((tok, head), BF16),
            pltpu.VMEM((1, tok), F32),
            pltpu.VMEM((tok, head), BF16),
            pltpu.VMEM((tok, head), BF16),
            dma((5,)),
            dma((CHUNKS + 1,)),
            dma((max(m - 1, 1),)),
            dma((n, 2 * CHUNKS)),
            dma((n, m)),
            dma(()),
            dma((2,)),
            dma((n,)),
            dma(()),
            dma((n,)),
            dma(()),
            dma(()),
            dma(()),
            dma(()),
            pltpu.SemaphoreType.REGULAR,
            pltpu.SemaphoreType.REGULAR,
        ],
        compiler_params=pltpu.CompilerParams(collective_id=0, has_side_effects=True),
    )(video_start, span_len, keys[0], values[0], rates, queries[0], init_weights)
    out, final = pl.pallas_call(
        finish,
        out_shape=(
            jax.ShapeDtypeStruct((tok, head), BF16),
            jax.ShapeDtypeStruct((3, rows, hidden), F32),
        ),
        in_specs=[vm, vm],
        out_specs=(hbm, hbm),
        scratch_shapes=[pltpu.VMEM((3, rows, hidden), F32), dma((2,))],
    )(*[pltpu.with_memory_space_constraint(a, pltpu.VMEM) for a in (out, final)])
    return out[None], final[None]


def solution(mesh):
    in_specs = (
        P(("groups", "batch"), ("seq", "inner"), None),
        P(("groups", "batch"), ("seq", "inner"), None),
        P(("groups", "batch"), ("seq", "inner"), None),
        P(("groups", "batch"), ("seq", "inner")),
        P(("groups", "batch")),
        P(("groups", "batch"), "seq"),
        P(),
    )
    out_specs = (
        P(("groups", "batch"), ("seq", "inner"), None),
        P(("groups", "batch"), None, "seq", None),
    )
    return jax.shard_map(
        per_device, mesh=mesh, in_specs=in_specs, out_specs=out_specs, check_vma=False
    )
```

```python
import functools

import jax
import jax.numpy as jnp
from jax import lax
from jax.experimental import pallas as pl
from jax.experimental.pallas import tpu as pltpu
from jax.sharding import PartitionSpec as P

NS_STEPS = 5
CHUNKS = 2
CALL_AFTER = 1
QUERY_AFTER = 2
MESH = pl.DeviceIdType.MESH
step_size = 0.1
norm_eps = 1e-07
column_eps = 1e-06
half_root = 0.5**0.5
F32, BF16 = jnp.float32, jnp.bfloat16


def dot(a, b, ca, cb):
    return lax.dot_general(a, b, (((ca,), (cb,)), ((), ())), preferred_element_type=F32)


def sigmoid(g):
    return 0.5 + 0.5 * jnp.tanh(0.5 * g)


def apply_net(rows, w1, w3, w2):
    gate = dot(rows, w1, 1, 0)
    up = dot(rows, w3, 1, 0)
    hidden = (gate * sigmoid(gate) * up).astype(BF16)
    return dot(hidden, w2, 1, 1).astype(BF16)


def span_grads(k, nv, ws, scales):
    gate = dot(k, ws[0], 1, 0) * scales[0]
    up = dot(k, ws[1], 1, 0) * scales[1]
    back = dot(nv, ws[2], 1, 0) * scales[2]
    s = sigmoid(gate)
    active = gate * s
    hidden = (active * up).astype(BF16)
    d_up = (back * active).astype(BF16)
    d_gate = (back * up * (s + active - active * s)).astype(BF16)
    return [dot(k, d_gate, 0, 0), dot(k, d_up, 0, 0), dot(nv, hidden, 0, 0)]


def newton(grads):
    size = grads[0].shape[0]
    at = [lax.broadcasted_iota(jnp.int32, (size, size), d) for d in range(2)]
    eye = jnp.where(at[0] == at[1], 1.5, 0.0).astype(F32)
    xs = [g.astype(BF16) for g in grads]
    scales = [
        half_root / (jnp.sqrt(jnp.sum(g * g, keepdims=True)) + norm_eps) for g in grads
    ]
    factors = [(dot(x, x, 1, 1) * (s * s) - eye).astype(BF16) for x, s in zip(xs, scales)]
    ys = [dot(f, x, 1, 0) * s for f, x, s in zip(factors, xs, scales)]
    for unused in range(1, NS_STEPS):
        xs = [y.astype(BF16) for y in ys]
        factors = [(dot(x, x, 1, 1) - eye).astype(BF16) for x in xs]
        ys = [dot(f, x, 1, 0) for f, x in zip(factors, xs)]
    sign = -1.0 if NS_STEPS % 2 == 0 else 1.0
    return ys if sign > 0 else [-y for y in ys]


def kernel(
    n, m, nb, start_ref, len_ref, key_ref, value_ref, rate_ref, q_ref, init_ref, out_ref, final_ref,
    kv, queue, outs, halves, state, root, fin, val_v, rate_v, q_v, nv_v,
    in_sem, kv_send, twin_send, part_recv, kv_recv, pass_send, q_send, q_recv, h_send, h_recv, o_send, o_recv, f_send, f_recv,
    go, qgo,
):
    z, x, b = lax.axis_index("seq"), lax.axis_index("inner"), lax.axis_index("batch")
    tok, head = value_ref.shape
    rows = final_ref.shape[1]

    def home(v):
        return (n // 2) * (1 - lax.rem(v, 2))

    other = lax.rem(b + 1, nb)
    served = lax.rem(b + nb - 1, nb)
    mz, sz = home(b), home(served)
    is_master, is_server = z == mz, z == sz
    is_source = jnp.logical_not(is_master)
    upper = z > mz

    def same_side(lower):
        return (lower >= 0) & (lower + 1 < n) & ((lower + 1 < mz) | (lower > mz))

    has_next, has_prev = same_side(z), same_side(z - 1)
    twins = [lax.rem(x + d, m) for d in range(1, m)]

    barrier = pltpu.get_barrier_semaphore()

    def greet(where):
        pl.semaphore_signal(barrier, inc=1, device_id=where, device_id_type=MESH)

    @pl.when(is_master)
    def _():
        for r in twins:
            greet({"inner": r})
        for r in range(m):
            greet({"inner": r, "batch": other})

    @pl.when(is_server)
    def _():
        @pl.loop(0, n)
        def _(c):
            greet({"seq": c, "batch": served})

    pl.when(has_prev)(lambda: greet({"seq": z - 1}))
    many = mz + 2 < n
    is_first, is_last = upper & many & (z == mz + 1), upper & many & (z == n - 1)
    holds_last = upper & many & (z == n - 2)
    pl.when(is_first)(lambda: greet({"seq": n - 1}))

    def fetch(src, dst, i):
        return pltpu.make_async_copy(src, dst, in_sem.at[i])

    get_val = fetch(value_ref, val_v, 0)
    get_rate = fetch(rate_ref, rate_v, 1)
    get_q = fetch(q_ref, q_v, 2)
    get_init = fetch(init_ref, state, 3)
    get_key = fetch(key_ref, kv.at[mz, x, 0], 4)
    get_rate.start()
    get_val.start()
    pl.when(is_master)(get_key.start)
    pl.when(z == 0)(get_q.start)
    pl.when((z == 0) | is_master)(get_init.start)

    pl.semaphore_wait(
        barrier,
        1
        + is_master.astype(jnp.int32) * (m - 1)
        + is_server.astype(jnp.int32) * m
        + has_next.astype(jnp.int32)
        + is_last.astype(jnp.int32),
    )

    def copy(src, dst, send, recv, where):
        return pltpu.make_async_remote_copy(src, dst, send, recv, where, MESH)

    pieces = 2 * CHUNKS
    part = tok // CHUNKS

    def piece(c, r, j):
        return kv.at[c, r, j // CHUNKS, pl.ds(j % CHUNKS * part, part)]

    def own_piece(j):
        return (key_ref if j < CHUNKS else nv_v).at[pl.ds(j % CHUNKS * part, part)]

    def give(j):
        send = kv_send.at[min(j, CHUNKS)]
        return copy(own_piece(j), piece(z, x, j), send, part_recv.at[z, j], server)

    def sent(j):
        return give(j) if j < CHUNKS else copy(nv_v, nv_v, kv_send.at[j], part_recv.at[z, j], server)

    def give_twin(j, d):
        where = {"inner": twins[d]}
        return copy(own_piece(j), piece(z, x, j), twin_send.at[d], kv_recv.at[z, x], where)

    def take_piece(c, j):
        return copy(piece(c, x, j), piece(c, x, j), pass_send, part_recv.at[c, j], server)

    def take(c, r, send=None):
        block = kv.at[c, r]
        return copy(block, block, twin_send.at[0] if send is None else send, kv_recv.at[c, r], server)

    def forward(c, j, r):
        where = {"inner": r, "batch": served}
        block = piece(c, x, j)
        return copy(block, block, pass_send, kv_recv.at[c, x], where)

    server = {"seq": mz, "batch": other}

    def give_query(h):
        half = pl.ds(h * (tok // 2), tok // 2)
        return copy(q_ref.at[half], queue.at[z, half], q_send.at[h], q_recv.at[z], server)

    def give_queries():
        for h in range(2):
            give_query(h).start()

    def give_half(c):
        return copy(halves.at[c], halves.at[c], h_send, h_recv.at[c], server)

    def give_out(c):
        where = {"seq": c, "batch": served}
        return copy(outs.at[c], out_ref, o_send, o_recv, where)

    def give_final(c, i):
        mine = pl.ds(pl.multiple_of(c * rows, rows), rows)
        return copy(fin.at[i, mine], final_ref.at[i], f_send, f_recv, {"seq": c})

    def call_next():
        pl.semaphore_signal(go, inc=1, device_id={"seq": z + 1}, device_id_type=MESH)

    @pl.when(is_source)
    def _():
        pl.when(has_prev)(lambda: pl.semaphore_wait(go, 1))
        for j in range(CHUNKS):
            give(j).start()

    @pl.when(is_master)
    def _():
        for d, r in enumerate(twins):
            for j in range(CHUNKS):
                give_twin(j, d).start()

    within = lax.broadcasted_iota(jnp.int32, (1, tok), 1) + x * tok
    position = within + z * (tok * m)
    eye = lax.broadcasted_iota(jnp.int32, (tok, tok), 0) == lax.broadcasted_iota(
        jnp.int32, (tok, tok), 1
    )
    get_rate.wait()
    valid = ((position >= start_ref[0]) & (within < len_ref[0, 0])).astype(F32)
    weight = rate_v[...] * valid
    column = jnp.sum(jnp.where(eye, weight, 0.0), axis=1, keepdims=True)
    get_val.wait()
    nv_v[...] = (-(column * val_v[...].astype(F32))).astype(BF16)

    @pl.when(is_source)
    def _():
        for j in range(CHUNKS, pieces):
            give(j).start()
        for j in range(CALL_AFTER):
            sent(j).wait_send()
        pl.when(has_next)(call_next)
        pl.when((z > 0) & jnp.logical_not(upper))(give_queries)

    @pl.when(is_master)
    def _():
        for d, r in enumerate(twins):
            for j in range(CHUNKS, pieces):
                give_twin(j, d).start()
        pl.when(z > 0)(give_queries)

    pl.when((z == 0) | is_master)(get_init.wait)

    @pl.when(z == 0)
    def _():
        get_q.wait()
        out_ref[...] = apply_net(q_v[...], *[state[i].astype(BF16) for i in range(3)])

    def sums(i):
        w = state[i]
        after = jnp.sum(w * w, axis=0, keepdims=True)
        scale = root[i] * lax.rsqrt(after + column_eps)
        total = after * (scale * scale) + column_eps
        root[i] = total * lax.rsqrt(total)
        return scale

    @pl.when(is_server)
    def _():
        @pl.loop(0, n)
        def _(c):
            @pl.when(c != sz)
            def _():
                for j in range(pieces):
                    take_piece(c, j).wait_recv()
                    for r in twins + [x]:
                        forward(c, j, r).start()

    def call_query(where):
        pl.semaphore_signal(qgo, inc=1, device_id={"seq": where}, device_id_type=MESH)

    @pl.when(is_source & upper)
    def _():
        @pl.when(is_last)
        def _():
            for j in range(CALL_AFTER, QUERY_AFTER):
                sent(j).wait_send()
            call_query(mz + 1)

        pl.when(many)(lambda: pl.semaphore_wait(qgo, 1))
        give_queries()
        pl.when(holds_last)(lambda: give_query(0).wait_send())
        pl.when(has_next)(lambda: call_query(z + 1))

    @pl.when(is_master)
    def _():
        for i in range(3):
            w = state[i]
            root[i] = jnp.sqrt(jnp.sum(w * w, axis=0, keepdims=True) + column_eps)
        kv[mz, x, 1] = nv_v[...]
        get_key.wait()

        def train(c, last):
            for d in range(m):
                r = lax.rem(x + d, m)
                pl.when((c != mz) | (r != x))(lambda: take(c, r).wait_recv())
            scales = [sums(i) for i in range(3)]
            ws = [state[i].astype(BF16) for i in range(3)]
            for i in range(3):
                w = state[i] * scales[i]
                state[i] = w
                halves[c, i] = w.astype(BF16)
            k = kv[c, :, 0].reshape(m * tok, head)
            nv = kv[c, :, 1].reshape(m * tok, head)
            grads = span_grads(k, nv, ws, scales)
            if last:
                give_half(c).start()
            for i, y in enumerate(newton(grads)):
                state[i] = state[i] + (step_size / half_root) * y
            if not last:
                pl.when(c > 0)(lambda: give_half(c).start())

        pl.loop(0, n - 1)(lambda c: train(c, False))
        train(n - 1, True)

        far = jnp.where(mz < n // 2, n - 1, 0)
        for i in range(3):
            fin[i] = (state[i] * sums(i)).astype(BF16)
            give_final(far, i).start()

        @pl.loop(1, n)
        def _(d):
            c = jnp.where(mz < n // 2, n - 1 - d, d)
            for i in range(3):
                pl.when(c != mz)(lambda: give_final(c, i).start())

        mine = pl.ds(pl.multiple_of(z * rows, rows), rows)
        final_ref[...] = fin[:, mine, :]

        rest = fin.at[:, pl.ds(0, (n - 1) * rows)]
        copy(rest, rest, f_send, f_recv, server).wait_send()
        rest = halves.at[pl.ds(1, n - 1)]
        copy(rest, rest, h_send, h_recv.at[0], server).wait_send()
        for d, r in enumerate(twins):
            take(z, x, twin_send.at[d]).wait_send()

    @pl.when(is_server)
    def _():
        @pl.loop(1, n)
        def _(c):
            copy(queue.at[c], queue.at[c], q_send.at[0], q_recv.at[c], server).wait_recv()
            give_half(c).wait_recv()
            outs[c] = apply_net(queue[c], *[halves[c, i] for i in range(3)])
            give_out(c).start()

        rest = outs.at[pl.ds(1, n - 1)]
        copy(rest, rest, o_send, o_recv, server).wait_send()
        rest = kv.at[pl.ds(0, n - 1)]
        copy(rest, rest, pass_send, kv_recv.at[0, 0], server).wait_send()

    @pl.when(is_source)
    def _():
        for j in range(CALL_AFTER, QUERY_AFTER):
            pl.when(jnp.logical_not(is_last))(sent(j).wait_send)
        for j in range(QUERY_AFTER, CHUNKS + 1):
            sent(j).wait_send()
        copy(final_ref, final_ref, f_send, f_recv, {"seq": 0}).wait_recv()

    @pl.when(z > 0)
    def _():
        pl.when(jnp.logical_not(holds_last))(lambda: give_query(0).wait_send())
        give_query(1).wait_send()
        give_out(0).wait_recv()


def finish(out_ref, final_ref, out_hbm, final_hbm, wide, sem):
    first = pltpu.make_async_copy(out_ref, out_hbm, sem.at[0])
    first.start()
    wide[...] = final_ref[...].astype(F32)
    second = pltpu.make_async_copy(wide, final_hbm, sem.at[1])
    second.start()
    first.wait()
    second.wait()


def per_device(queries, keys, values, rates, video_start, span_len, init_weights):
    tok, head = queries.shape[1:]
    n, m, nb = lax.axis_size("seq"), lax.axis_size("inner"), lax.axis_size("batch")
    hidden = init_weights.shape[2]
    rows = init_weights.shape[1] // n
    vm = pl.BlockSpec(memory_space=pltpu.VMEM)
    hbm = pl.BlockSpec(memory_space=pl.ANY)
    dma = pltpu.SemaphoreType.DMA
    out, final = pl.pallas_call(
        functools.partial(kernel, n, m, nb),
        out_shape=(
            pltpu.VMEM((tok, head), BF16),
            pltpu.VMEM((3, rows, hidden), BF16),
        ),
        in_specs=[pl.BlockSpec(memory_space=pltpu.SMEM)] * 2 + [hbm] * 5,
        out_specs=(vm, vm),
        scratch_shapes=[
            pltpu.VMEM((n, m, 2, tok, head), BF16),
            pltpu.VMEM((n, tok, head), BF16),
            pltpu.VMEM((n, tok, head), BF16),
            pltpu.VMEM((n,) + init_weights.shape, BF16),
            pltpu.VMEM(init_weights.shape, F32),
            pltpu.VMEM((3, 1, hidden), F32),
            pltpu.VMEM(init_weights.shape, BF16),
            pltpu.VMEM((tok, head), BF16),
            pltpu.VMEM((1, tok), F32),
            pltpu.VMEM((tok, head), BF16),
            pltpu.VMEM((tok, head), BF16),
            dma((5,)),
            dma((CHUNKS + 1,)),
            dma((max(m - 1, 1),)),
            dma((n, 2 * CHUNKS)),
            dma((n, m)),
            dma(()),
            dma((2,)),
            dma((n,)),
            dma(()),
            dma((n,)),
            dma(()),
            dma(()),
            dma(()),
            dma(()),
            pltpu.SemaphoreType.REGULAR,
            pltpu.SemaphoreType.REGULAR,
        ],
        compiler_params=pltpu.CompilerParams(collective_id=0, has_side_effects=True),
    )(video_start, span_len, keys[0], values[0], rates, queries[0], init_weights)
    out, final = pl.pallas_call(
        finish,
        out_shape=(
            jax.ShapeDtypeStruct((tok, head), BF16),
            jax.ShapeDtypeStruct((3, rows, hidden), F32),
        ),
        in_specs=[vm, vm],
        out_specs=(hbm, hbm),
        scratch_shapes=[pltpu.VMEM((3, rows, hidden), F32), dma((2,))],
    )(*[pltpu.with_memory_space_constraint(a, pltpu.VMEM) for a in (out, final)])
    return out[None], final[None]


def solution(mesh):
    in_specs = (
        P(("groups", "batch"), ("seq", "inner"), None),
        P(("groups", "batch"), ("seq", "inner"), None),
        P(("groups", "batch"), ("seq", "inner"), None),
        P(("groups", "batch"), ("seq", "inner")),
        P(("groups", "batch")),
        P(("groups", "batch"), "seq"),
        P(),
    )
    out_specs = (
        P(("groups", "batch"), ("seq", "inner"), None),
        P(("groups", "batch"), None, "seq", None),
    )
    return jax.shard_map(
        per_device, mesh=mesh, in_specs=in_specs, out_specs=out_specs, check_vma=False
    )
```

```python
import functools

import jax
import jax.numpy as jnp
from jax import lax
from jax.experimental import pallas as pl
from jax.experimental.pallas import tpu as pltpu
from jax.sharding import PartitionSpec as P

NS_STEPS = 5
CHUNKS = 4
CALL_AFTER = 2
QUERY_AFTER = 4
MESH = pl.DeviceIdType.MESH
step_size = 0.1
norm_eps = 1e-07
column_eps = 1e-06
half_root = 0.5**0.5
F32, BF16 = jnp.float32, jnp.bfloat16


def dot(a, b, ca, cb):
    return lax.dot_general(a, b, (((ca,), (cb,)), ((), ())), preferred_element_type=F32)


def sigmoid(g):
    return 0.5 + 0.5 * jnp.tanh(0.5 * g)


def apply_net(rows, w1, w3, w2):
    gate = dot(rows, w1, 1, 0)
    up = dot(rows, w3, 1, 0)
    hidden = (gate * sigmoid(gate) * up).astype(BF16)
    return dot(hidden, w2, 1, 1).astype(BF16)


def span_grads(k, nv, ws, scales):
    gate = dot(k, ws[0], 1, 0) * scales[0]
    up = dot(k, ws[1], 1, 0) * scales[1]
    back = dot(nv, ws[2], 1, 0) * scales[2]
    s = sigmoid(gate)
    active = gate * s
    hidden = (active * up).astype(BF16)
    d_up = (back * active).astype(BF16)
    d_gate = (back * up * (s + active - active * s)).astype(BF16)
    return [dot(k, d_gate, 0, 0), dot(k, d_up, 0, 0), dot(nv, hidden, 0, 0)]


def newton(grads):
    size = grads[0].shape[0]
    at = [lax.broadcasted_iota(jnp.int32, (size, size), d) for d in range(2)]
    eye = jnp.where(at[0] == at[1], 1.5, 0.0).astype(F32)
    xs = [g.astype(BF16) for g in grads]
    scales = [
        half_root / (jnp.sqrt(jnp.sum(g * g, keepdims=True)) + norm_eps) for g in grads
    ]
    factors = [(dot(x, x, 1, 1) * (s * s) - eye).astype(BF16) for x, s in zip(xs, scales)]
    ys = [dot(f, x, 1, 0) * s for f, x, s in zip(factors, xs, scales)]
    for unused in range(1, NS_STEPS):
        xs = [y.astype(BF16) for y in ys]
        factors = [(dot(x, x, 1, 1) - eye).astype(BF16) for x in xs]
        ys = [dot(f, x, 1, 0) for f, x in zip(factors, xs)]
    sign = -1.0 if NS_STEPS % 2 == 0 else 1.0
    return ys if sign > 0 else [-y for y in ys]


def kernel(
    n, m, nb, start_ref, len_ref, key_ref, value_ref, rate_ref, q_ref, init_ref, out_ref, final_ref,
    kv, queue, outs, halves, state, root, grad, fin, val_v, rate_v, q_v, nv_v,
    in_sem, kv_send, twin_send, part_recv, kv_recv, pass_send, q_send, q_recv, h_send, h_recv, o_send, o_recv, f_send, f_recv,
    go, qgo,
):
    z, x, b = lax.axis_index("seq"), lax.axis_index("inner"), lax.axis_index("batch")
    tok, head = value_ref.shape
    rows = final_ref.shape[1]

    def home(v):
        return (n // 2) * (1 - lax.rem(v, 2))

    other = lax.rem(b + 1, nb)
    served = lax.rem(b + nb - 1, nb)
    mz, sz = home(b), home(served)
    is_master, is_server = z == mz, z == sz
    is_source = jnp.logical_not(is_master)
    upper = z > mz

    def same_side(lower):
        return (lower >= 0) & (lower + 1 < n) & ((lower + 1 < mz) | (lower > mz))

    has_next, has_prev = same_side(z), same_side(z - 1)
    twins = [lax.rem(x + d, m) for d in range(1, m)]

    barrier = pltpu.get_barrier_semaphore()

    def greet(where):
        pl.semaphore_signal(barrier, inc=1, device_id=where, device_id_type=MESH)

    @pl.when(is_master)
    def _():
        for r in twins:
            greet({"inner": r})
        for r in range(m):
            greet({"inner": r, "batch": other})

    @pl.when(is_server)
    def _():
        @pl.loop(0, n)
        def _(c):
            greet({"seq": c, "batch": served})

    pl.when(has_prev)(lambda: greet({"seq": z - 1}))
    many = mz + 2 < n
    is_first, is_last = upper & many & (z == mz + 1), upper & many & (z == n - 1)
    holds_last = upper & many & (z == n - 2)
    pl.when(is_first)(lambda: greet({"seq": n - 1}))

    def fetch(src, dst, i):
        return pltpu.make_async_copy(src, dst, in_sem.at[i])

    get_val = fetch(value_ref, val_v, 0)
    get_rate = fetch(rate_ref, rate_v, 1)
    get_q = fetch(q_ref, q_v, 2)
    get_init = fetch(init_ref, state, 3)
    get_key = fetch(key_ref, kv.at[mz, x, 0], 4)
    get_rate.start()
    get_val.start()
    pl.when(is_master)(get_key.start)
    pl.when(z == 0)(get_q.start)
    pl.when((z == 0) | is_master)(get_init.start)

    within = lax.broadcasted_iota(jnp.int32, (1, tok), 1) + x * tok
    position = within + z * (tok * m)
    eye = lax.broadcasted_iota(jnp.int32, (tok, tok), 0) == lax.broadcasted_iota(
        jnp.int32, (tok, tok), 1
    )
    get_rate.wait()
    valid = ((position >= start_ref[0]) & (within < len_ref[0, 0])).astype(F32)
    weight = rate_v[...] * valid
    column = jnp.sum(jnp.where(eye, weight, 0.0), axis=1, keepdims=True)
    get_val.wait()
    nv_v[...] = (-(column * val_v[...].astype(F32))).astype(BF16)

    pl.semaphore_wait(
        barrier,
        1
        + is_master.astype(jnp.int32) * (m - 1)
        + is_server.astype(jnp.int32) * m
        + has_next.astype(jnp.int32)
        + is_last.astype(jnp.int32),
    )

    def copy(src, dst, send, recv, where):
        return pltpu.make_async_remote_copy(src, dst, send, recv, where, MESH)

    pieces = 2 * CHUNKS
    part = tok // CHUNKS

    def piece(c, r, j):
        return kv.at[c, r, j // CHUNKS, pl.ds(j % CHUNKS * part, part)]

    def own_piece(j):
        return (key_ref if j < CHUNKS else nv_v).at[pl.ds(j % CHUNKS * part, part)]

    def give(j):
        send = kv_send.at[min(j, CHUNKS)]
        return copy(own_piece(j), piece(z, x, j), send, part_recv.at[z, j], server)

    def sent(j):
        return give(j) if j < CHUNKS else copy(nv_v, nv_v, kv_send.at[j], part_recv.at[z, j], server)

    def give_twin(j, d):
        where = {"inner": twins[d]}
        return copy(own_piece(j), piece(z, x, j), twin_send.at[d], kv_recv.at[z, x], where)

    def take_piece(c, j):
        return copy(piece(c, x, j), piece(c, x, j), pass_send, part_recv.at[c, j], server)

    def take(c, r, send=None):
        block = kv.at[c, r]
        return copy(block, block, twin_send.at[0] if send is None else send, kv_recv.at[c, r], server)

    def forward(c, j, r):
        where = {"inner": r, "batch": served}
        block = piece(c, x, j)
        return copy(block, block, pass_send, kv_recv.at[c, x], where)

    server = {"seq": mz, "batch": other}

    def give_query(h):
        half = pl.ds(h * (tok // 2), tok // 2)
        return copy(q_ref.at[half], queue.at[z, half], q_send.at[h], q_recv.at[z], server)

    def give_queries():
        for h in range(2):
            give_query(h).start()

    def give_half(c):
        return copy(halves.at[c], halves.at[c], h_send, h_recv.at[c], server)

    def give_out(c):
        where = {"seq": c, "batch": served}
        return copy(outs.at[c], out_ref, o_send, o_recv, where)

    def give_final(c, i):
        mine = pl.ds(pl.multiple_of(c * rows, rows), rows)
        return copy(fin.at[i, mine], final_ref.at[i], f_send, f_recv, {"seq": c})

    def call_next():
        pl.semaphore_signal(go, inc=1, device_id={"seq": z + 1}, device_id_type=MESH)

    @pl.when(is_source)
    def _():
        pl.when(has_prev)(lambda: pl.semaphore_wait(go, 1))
        for j in range(pieces):
            give(j).start()
        for j in range(CALL_AFTER):
            sent(j).wait_send()
        pl.when(has_next)(call_next)
        pl.when((z > 0) & jnp.logical_not(upper))(give_queries)

    @pl.when(is_master)
    def _():
        for d, r in enumerate(twins):
            for j in range(pieces):
                give_twin(j, d).start()
        pl.when(z > 0)(give_queries)

    pl.when((z == 0) | is_master)(get_init.wait)

    @pl.when(z == 0)
    def _():
        get_q.wait()
        out_ref[...] = apply_net(q_v[...], *[state[i].astype(BF16) for i in range(3)])

    def sums(i):
        w = state[i]
        after = jnp.sum(w * w, axis=0, keepdims=True)
        scale = root[i] * lax.rsqrt(after + column_eps)
        total = after * (scale * scale) + column_eps
        root[i] = total * lax.rsqrt(total)
        return scale

    @pl.when(is_server)
    def _():
        @pl.loop(0, n)
        def _(c):
            @pl.when(c != sz)
            def _():
                for j in range(pieces):
                    take_piece(c, j).wait_recv()
                    for r in twins + [x]:
                        forward(c, j, r).start()

    def call_query(where):
        pl.semaphore_signal(qgo, inc=1, device_id={"seq": where}, device_id_type=MESH)

    @pl.when(is_source & upper)
    def _():
        @pl.when(is_last)
        def _():
            for j in range(CALL_AFTER, QUERY_AFTER):
                sent(j).wait_send()
            call_query(mz + 1)

        pl.when(many)(lambda: pl.semaphore_wait(qgo, 1))
        give_queries()
        pl.when(holds_last)(lambda: give_query(0).wait_send())
        pl.when(has_next)(lambda: call_query(z + 1))

    @pl.when(is_master)
    def _():
        for i in range(3):
            w = state[i]
            root[i] = jnp.sqrt(jnp.sum(w * w, axis=0, keepdims=True) + column_eps)
        kv[mz, x, 1] = nv_v[...]
        get_key.wait()

        def train(c, last):
            for d in range(m):
                r = lax.rem(x + d, m)
                pl.when((c != mz) | (r != x))(lambda: take(c, r).wait_recv())
            scales = [sums(i) for i in range(3)]
            ws = [state[i].astype(BF16) for i in range(3)]
            for i in range(3):
                w = state[i] * scales[i]
                state[i] = w
                halves[c, i] = w.astype(BF16)
            k = kv[c, :, 0].reshape(m * tok, head)
            nv = kv[c, :, 1].reshape(m * tok, head)
            grads = span_grads(k, nv, ws, scales)
            if last:
                for i in range(3):
                    grad[i] = grads[i]
                give_half(c).start()
                grads = [grad[i] for i in range(3)]
            for i, y in enumerate(newton(grads)):
                state[i] = state[i] + (step_size / half_root) * y
            if not last:
                pl.when(c > 0)(lambda: give_half(c).start())

        pl.loop(0, n - 1)(lambda c: train(c, False))
        train(n - 1, True)

        far = jnp.where(mz < n // 2, n - 1, 0)
        for i in range(3):
            fin[i] = (state[i] * sums(i)).astype(BF16)
            give_final(far, i).start()

        @pl.loop(1, n)
        def _(d):
            c = jnp.where(mz < n // 2, n - 1 - d, d)
            for i in range(3):
                pl.when(c != mz)(lambda: give_final(c, i).start())

        mine = pl.ds(pl.multiple_of(z * rows, rows), rows)
        final_ref[...] = fin[:, mine, :]

        rest = fin.at[:, pl.ds(0, (n - 1) * rows)]
        copy(rest, rest, f_send, f_recv, server).wait_send()
        rest = halves.at[pl.ds(1, n - 1)]
        copy(rest, rest, h_send, h_recv.at[0], server).wait_send()
        for d, r in enumerate(twins):
            take(z, x, twin_send.at[d]).wait_send()

    @pl.when(is_server)
    def _():
        @pl.loop(1, n)
        def _(c):
            copy(queue.at[c], queue.at[c], q_send.at[0], q_recv.at[c], server).wait_recv()
            give_half(c).wait_recv()
            outs[c] = apply_net(queue[c], *[halves[c, i] for i in range(3)])
            give_out(c).start()

        rest = outs.at[pl.ds(1, n - 1)]
        copy(rest, rest, o_send, o_recv, server).wait_send()
        rest = kv.at[pl.ds(0, n - 1)]
        copy(rest, rest, pass_send, kv_recv.at[0, 0], server).wait_send()

    @pl.when(is_source)
    def _():
        for j in range(CALL_AFTER, QUERY_AFTER):
            pl.when(jnp.logical_not(is_last))(sent(j).wait_send)
        for j in range(QUERY_AFTER, CHUNKS + 1):
            sent(j).wait_send()
        copy(final_ref, final_ref, f_send, f_recv, {"seq": 0}).wait_recv()

    @pl.when(z > 0)
    def _():
        pl.when(jnp.logical_not(holds_last))(lambda: give_query(0).wait_send())
        give_query(1).wait_send()
        give_out(0).wait_recv()


def finish(out_ref, final_ref, out_hbm, final_hbm, wide, sem):
    first = pltpu.make_async_copy(out_ref, out_hbm, sem.at[0])
    first.start()
    wide[...] = final_ref[...].astype(F32)
    second = pltpu.make_async_copy(wide, final_hbm, sem.at[1])
    second.start()
    first.wait()
    second.wait()


def per_device(queries, keys, values, rates, video_start, span_len, init_weights):
    tok, head = queries.shape[1:]
    n, m, nb = lax.axis_size("seq"), lax.axis_size("inner"), lax.axis_size("batch")
    hidden = init_weights.shape[2]
    rows = init_weights.shape[1] // n
    vm = pl.BlockSpec(memory_space=pltpu.VMEM)
    hbm = pl.BlockSpec(memory_space=pl.ANY)
    dma = pltpu.SemaphoreType.DMA
    out, final = pl.pallas_call(
        functools.partial(kernel, n, m, nb),
        out_shape=(
            pltpu.VMEM((tok, head), BF16),
            pltpu.VMEM((3, rows, hidden), BF16),
        ),
        in_specs=[pl.BlockSpec(memory_space=pltpu.SMEM)] * 2 + [hbm] * 5,
        out_specs=(vm, vm),
        scratch_shapes=[
            pltpu.VMEM((n, m, 2, tok, head), BF16),
            pltpu.VMEM((n, tok, head), BF16),
            pltpu.VMEM((n, tok, head), BF16),
            pltpu.VMEM((n,) + init_weights.shape, BF16),
            pltpu.VMEM(init_weights.shape, F32),
            pltpu.VMEM((3, 1, hidden), F32),
            pltpu.VMEM(init_weights.shape, F32),
            pltpu.VMEM(init_weights.shape, BF16),
            pltpu.VMEM((tok, head), BF16),
            pltpu.VMEM((1, tok), F32),
            pltpu.VMEM((tok, head), BF16),
            pltpu.VMEM((tok, head), BF16),
            dma((5,)),
            dma((CHUNKS + 1,)),
            dma((max(m - 1, 1),)),
            dma((n, 2 * CHUNKS)),
            dma((n, m)),
            dma(()),
            dma((2,)),
            dma((n,)),
            dma(()),
            dma((n,)),
            dma(()),
            dma(()),
            dma(()),
            dma(()),
            pltpu.SemaphoreType.REGULAR,
            pltpu.SemaphoreType.REGULAR,
        ],
        compiler_params=pltpu.CompilerParams(collective_id=0, has_side_effects=True),
    )(video_start, span_len, keys[0], values[0], rates, queries[0], init_weights)
    out, final = pl.pallas_call(
        finish,
        out_shape=(
            jax.ShapeDtypeStruct((tok, head), BF16),
            jax.ShapeDtypeStruct((3, rows, hidden), F32),
        ),
        in_specs=[vm, vm],
        out_specs=(hbm, hbm),
        scratch_shapes=[pltpu.VMEM((3, rows, hidden), F32), dma((2,))],
    )(*[pltpu.with_memory_space_constraint(a, pltpu.VMEM) for a in (out, final)])
    return out[None], final[None]


def solution(mesh):
    in_specs = (
        P(("groups", "batch"), ("seq", "inner"), None),
        P(("groups", "batch"), ("seq", "inner"), None),
        P(("groups", "batch"), ("seq", "inner"), None),
        P(("groups", "batch"), ("seq", "inner")),
        P(("groups", "batch")),
        P(("groups", "batch"), "seq"),
        P(),
    )
    out_specs = (
        P(("groups", "batch"), ("seq", "inner"), None),
        P(("groups", "batch"), None, "seq", None),
    )
    return jax.shard_map(
        per_device, mesh=mesh, in_specs=in_specs, out_specs=out_specs, check_vma=False
    )
```
